128 devices in a mesh: sub: 16 (over y, x), front: 8 (over z, core).
Axes of the slice: x: 4, y: 4, z: 4, core: 2. Of those that a mesh axis runs over, the one named last changes fastest.
Arguments:
- front_inverse: bfloat16 [16, 16384, 2048], P('sub', 'front'), may hold values from -0.75 to 0.75
- coupling: bfloat16 [16, 16384, 2048], P('sub', 'front'), may hold values from -0.0234375 to 0.0234375
- free_modes: bfloat16 [16, 300, 16384], P('sub', None, 'front'), may hold values from -0.09375 to 0.09375
- dof_offset: int32 [16, 256], P('sub', 'front'), may hold values from 0 to 2047, as said below
- interface_id: int32 [16, 256], replicated, may hold values from 0 to 2047, as said below
Outputs:
- attachment: bfloat16 [16, 256, 16384], P('sub', None, 'front')
- flexibility: float32 [2048, 2048], P(('sub', 'front'))
The draws below stay inside these ranges and needn't reach their ends.
Inputs may be any that keep to these rules, and one draw needn't show every extreme that they name: `dof_offset`: within one substructure and one front the 32 offsets are distinct, and 0 and 2047 occur among them. `interface_id`: every value occurs exactly twice in the whole array.
All inputs are finite; a program needn't handle non-finite values.
Results may differ from the reference program's by a relative error of at most 0.02.
Values may be sent and summed in bfloat16 or wider, within the bound.
A program may use at most 128 MiB of HBM per device.

```python
import jax
import jax.numpy as jnp
from jax import lax

NF = 2048
M = 300
RHS = 256
SUBS = 16
FRONTS = 8
NTOT = 16384
RJ = 32
NI = 2048
N_FRONT = 8


def draw_dof_offset(key, part):
    keys = jax.random.split(key, SUBS * FRONTS)

    def one_block(block_key):
        first_key, second_key = jax.random.split(block_key)
        inner = (jax.random.permutation(first_key, NF - 2)[:RJ - 2] + 1).astype(jnp.int32)
        values = jnp.concatenate([jnp.array([0, NF - 1], jnp.int32), inner])
        return jax.random.permutation(second_key, values)
    return jax.vmap(one_block)(keys).reshape(SUBS, RHS).astype(jnp.int32)


def draw_interface_id(key, part):
    values = jnp.arange(SUBS * RHS, dtype=jnp.int32) // 2
    return jax.random.permutation(key, values).reshape(SUBS, RHS).astype(jnp.int32)


def block_scale(own_key, dims, shards, least, top_value):
    def one(position, parts):
        draws = jax.random.uniform(jax.random.fold_in(jax.random.fold_in(own_key, 6), position), (parts,), jnp.float32, least / len(shards), top_value / len(shards))
        return jnp.repeat(jnp.exp(draws), dims[position] // parts).reshape((-1,) + (1,) * (len(dims) - position - 1))

    level = one(*shards[0])
    for cut in shards[1:]:
        level = level * one(*cut)
    return level


def bell_draw(own_key, extent, width, limit, shards=(), kind=jnp.bfloat16):
    values = jax.random.normal(own_key, extent, jnp.float32) * width
    if len(shards) > 0:
        values = block_scale(own_key, extent, shards, -0.22, 0.18) * values
    return jnp.clip(values, min=-limit, max=limit).astype(kind)


def setup_inputs(seed: int = 0) -> dict:
    arg_keys = jax.random.split(jax.random.key(seed), 6)
    return {
        "front_inverse": bell_draw(arg_keys[0], (SUBS, NTOT, NF), (NF // 32) ** -0.5, 0.75, ((0, 16), (1, 8))),
        "coupling": bell_draw(arg_keys[1], (SUBS, NTOT, NF), (32 * NF) ** -0.5, 0.0234375, ((0, 16), (1, 8))),
        "free_modes": bell_draw(arg_keys[2], (SUBS, M, NTOT), (NF * N_FRONT // 4) ** -0.5, 0.09375, ((0, 16), (2, 8))),
        "dof_offset": draw_dof_offset(jax.random.fold_in(arg_keys[5], 71), 0),
        "interface_id": draw_interface_id(jax.random.fold_in(arg_keys[5], 71), 0),
    }


def contract_last(left, right):
    return lax.dot_general(left, right, (((1,), (1,)), ((), ())), preferred_element_type=jnp.float32)


def reference(front_inverse, coupling, free_modes, dof_offset, interface_id):
    column_ids = jnp.arange(RHS, dtype=jnp.int32)
    row_ids = jnp.arange(NF, dtype=jnp.int32)
    dual_ids = jnp.arange(NI, dtype=jnp.int32)
    holder = column_ids // RJ

    def per_sub(flex, index):
        inverse_all = lax.dynamic_index_in_dim(front_inverse, index, 0, keepdims=False)
        coupling_all = lax.dynamic_index_in_dim(coupling, index, 0, keepdims=False)
        modes_all = lax.dynamic_index_in_dim(free_modes, index, 0, keepdims=False)
        offsets = lax.dynamic_index_in_dim(dof_offset, index, 0, keepdims=False).astype(jnp.int32)
        labels = lax.dynamic_index_in_dim(interface_id, index, 0, keepdims=False).astype(jnp.int32)
        forward_list = []
        previous = None
        for front in range(FRONTS):
            inverse_block = inverse_all[front * NF:(front + 1) * NF]
            coupling_block = coupling_all[front * NF:(front + 1) * NF]
            load = ((holder[:, None] == front) & (offsets[:, None] == row_ids[None, :])).astype(jnp.float32)
            if previous is not None:
                load = load - contract_last(previous, coupling_block)
            solved = contract_last(load.astype(jnp.bfloat16), inverse_block).astype(jnp.bfloat16)
            forward_list.append(solved)
            previous = solved
        backward_list = [None] * FRONTS
        passed = None
        for front in range(FRONTS - 1, -1, -1):
            inverse_block = inverse_all[front * NF:(front + 1) * NF]
            coupling_block = coupling_all[front * NF:(front + 1) * NF]
            upper = forward_list[front].astype(jnp.float32)
            if passed is not None:
                upper = upper - passed.astype(jnp.float32)
            moved = jnp.dot(upper.astype(jnp.bfloat16), inverse_block, preferred_element_type=jnp.float32)
            passed = jnp.dot(moved.astype(jnp.bfloat16), coupling_block, preferred_element_type=jnp.float32).astype(jnp.bfloat16)
            backward_list[front] = moved
        displacement = jnp.concatenate(backward_list, axis=1)
        modal = contract_last(displacement.astype(jnp.bfloat16), modes_all)
        deflated = displacement - jnp.dot(modal.astype(jnp.bfloat16), modes_all, preferred_element_type=jnp.float32)
        picked = (holder * NF + offsets).astype(jnp.int32)
        block = jnp.take(deflated, picked, axis=1).T
        placed = (labels[:, None] == dual_ids[None, :]).astype(jnp.float32)
        spread = jnp.dot(block, placed, precision=lax.Precision.HIGHEST)
        flex = flex + jnp.dot(placed.T, spread, precision=lax.Precision.HIGHEST)
        return flex, deflated.astype(jnp.bfloat16)

    flex, attachment = lax.scan(per_sub, jnp.zeros((NI, NI), jnp.float32), jnp.arange(SUBS, dtype=jnp.int32))
    return attachment, flex
```

```python
import functools

import jax
import jax.numpy as jnp
from jax import lax
from jax.experimental import pallas as pl
from jax.experimental.pallas import tpu as pltpu
from jax.sharding import PartitionSpec as P

MESH = pl.DeviceIdType.MESH
F32 = jnp.float32
BF16 = jnp.bfloat16

FRONTS = 8
SUBS = 16
NF = 2048
COLS = 256
OWN = 32
GROUPS = 4
WIDTH = 64
MODES = 300
MPAD = 384
SHARE = 16
HIGH = 5


def dot(left, right):
    return jnp.dot(left, right, preferred_element_type=F32)


def dot_last(left, right):
    return lax.dot_general(left, right, (((1,), (1,)), ((), ())), preferred_element_type=F32)


def tile(index, size):
    return pl.ds(pl.multiple_of(index * size, size), size)


def kernel(
    inverse_hbm,
    coupling_hbm,
    modes_hbm,
    offsets_ref,
    ids_ref,
    attachment_hbm,
    flexibility_hbm,
    inverse,
    coupling,
    modes_raw,
    modes,
    product,
    turned,
    coupling_turned,
    modal_map,
    pick,
    own,
    solved,
    solved_in,
    back,
    handed,
    handed_in,
    modal_out,
    modal_in,
    modal,
    mode_rows,
    entries,
    route,
    rows_out,
    rows_in,
    low_pick,
    displaced,
    attachment,
    flexibility,
    load_sem,
    fwd_send,
    fwd_recv,
    bwd_send,
    bwd_recv,
    sum_send,
    sum_recv,
    modal_send,
    modal_recv,
    mode_send,
    mode_recv,
    entry_send,
    entry_recv,
    row_send,
    row_recv,
    store_sem,
):
    front = lax.axis_index("front")
    sub = lax.axis_index("sub")
    high = front >= HIGH
    low = jnp.logical_and(front >= 1, front < HIGH)

    loads = [
        pltpu.make_async_copy(inverse_hbm.at[0], inverse, load_sem.at[0]),
        pltpu.make_async_copy(coupling_hbm.at[0], coupling, load_sem.at[1]),
        pltpu.make_async_copy(modes_hbm.at[0], modes_raw, load_sem.at[2]),
    ]
    for load in loads:
        load.start()

    def peer_front(step):
        return lax.rem(front + step, FRONTS)

    def peer_sub(step):
        return lax.rem(sub + step, SUBS)

    barrier = pltpu.get_barrier_semaphore()

    def greet_front(step, carry):
        pl.semaphore_signal(barrier, inc=1, device_id={"front": peer_front(step)}, device_id_type=MESH)
        return carry

    def greet_sub(step, carry):
        pl.semaphore_signal(barrier, inc=1, device_id={"sub": peer_sub(step)}, device_id_type=MESH)
        return carry

    lax.fori_loop(1, FRONTS, greet_front, 0)
    lax.fori_loop(1, SUBS, greet_sub, 0)

    offsets_square = jnp.broadcast_to(offsets_ref[...].astype(F32), (OWN, OWN))
    diagonal = lax.broadcasted_iota(jnp.int32, (OWN, OWN), 0) == lax.broadcasted_iota(
        jnp.int32, (OWN, OWN), 1
    )
    offsets_column = jnp.sum(
        jnp.where(diagonal, offsets_square, 0.0), axis=1, keepdims=True
    ).astype(jnp.int32)
    pick[...] = (offsets_column == lax.broadcasted_iota(jnp.int32, (OWN, NF), 1)).astype(F32).astype(BF16)
    place = lax.broadcasted_iota(jnp.int32, (COLS, COLS), 0)
    target = lax.shift_right_logical(place, 4) * (FRONTS * SHARE) + jnp.bitwise_and(place, 15) + front * SHARE
    route[...] = (target == ids_ref[pl.ds(sub, 1), :]).astype(F32).astype(BF16)
    lane_place = lax.broadcasted_iota(jnp.int32, (128, COLS), 0)

    def fill_low(index, carry):
        ids = jnp.bitwise_and(ids_ref[pl.ds(index, 1), :], 127)
        low_pick[index] = (lane_place == ids).astype(F32).astype(BF16)
        return carry

    lax.fori_loop(0, SUBS, fill_low, 0)
    solved[...] = jnp.zeros((COLS, NF), BF16)
    modes[...] = jnp.zeros((MPAD, NF), BF16)

    pl.semaphore_wait(barrier, FRONTS - 1 + SUBS - 1)

    def turn(source, destination):
        def one(index, carry):
            destination[:, tile(index, 512)] = source[tile(index, 512), :].T
            return carry

        lax.fori_loop(0, NF // 512, one, 0)

    loads[0].wait()

    @pl.when(jnp.logical_not(low))
    def _():
        def one(index, carry):
            own[:, tile(index, 512)] = dot_last(pick[...], inverse[tile(index, 512), :]).astype(BF16)
            return carry

        lax.fori_loop(0, NF // 512, one, 0)

    @pl.when(low)
    def _():
        turn(inverse, turned)

    loads[1].wait()

    @pl.when(low)
    def _():
        turn(coupling, coupling_turned)

        def one(index, carry):
            own[:, tile(index, 512)] = dot(pick[...], turned[:, tile(index, 512)]).astype(BF16)
            return carry

        lax.fori_loop(0, NF // 512, one, 0)

    own_start = pl.multiple_of(front * OWN, OWN)
    own_rows = pl.ds(own_start, OWN)
    solved[own_rows, :] = own[...]

    def copy_fwd(group):
        return pltpu.make_async_remote_copy(
            src_ref=solved.at[tile(group, WIDTH)],
            dst_ref=solved_in.at[group],
            send_sem=fwd_send.at[group],
            recv_sem=fwd_recv.at[group],
            device_id={"front": jnp.minimum(front + 1, FRONTS - 1)},
            device_id_type=MESH,
        )

    def copy_bwd(group):
        return pltpu.make_async_remote_copy(
            src_ref=handed.at[group],
            dst_ref=handed_in.at[group],
            send_sem=bwd_send.at[group],
            recv_sem=bwd_recv.at[group],
            device_id={"front": jnp.maximum(front - 1, 0)},
            device_id_type=MESH,
        )

    def copy_sum(group):
        return pltpu.make_async_remote_copy(
            src_ref=modal_out.at[group],
            dst_ref=modal_in.at[group],
            send_sem=sum_send.at[group],
            recv_sem=sum_recv.at[group],
            device_id={"front": jnp.maximum(front - 1, 0)},
            device_id_type=MESH,
        )

    def copy_modal(group, step):
        return pltpu.make_async_remote_copy(
            src_ref=modal.at[tile(group, WIDTH)],
            dst_ref=modal.at[tile(group, WIDTH)],
            send_sem=modal_send.at[group, step],
            recv_sem=modal_recv.at[group],
            device_id={"front": peer_front(step)},
            device_id_type=MESH,
        )

    def rows_of(buffer, sends, receives, step, index):
        rows = pl.ds(pl.multiple_of(index * OWN, OWN), OWN)
        return pltpu.make_async_remote_copy(
            src_ref=buffer.at[rows],
            dst_ref=buffer.at[rows],
            send_sem=sends.at[step],
            recv_sem=receives.at[index],
            device_id={"front": peer_front(step)},
            device_id_type=MESH,
        )

    def copy_mode(step, index):
        return rows_of(mode_rows, mode_send, mode_recv, step, index)

    def copy_entry(step, index):
        return rows_of(entries, entry_send, entry_recv, step, index)

    def copy_row(step, source):
        return pltpu.make_async_remote_copy(
            src_ref=rows_out.at[peer_sub(step)],
            dst_ref=rows_in.at[source],
            send_sem=row_send.at[step],
            recv_sem=row_recv.at[source],
            device_id={"sub": peer_sub(step)},
            device_id_type=MESH,
        )

    def build_maps():
        loads[2].wait()
        modes[pl.ds(0, MODES), :] = modes_raw[...]
        mode_rows[own_rows, :] = dot_last(pick[...], modes[...]).astype(BF16)

        def send(step, carry):
            copy_mode(step, front).start()
            return carry

        lax.fori_loop(1, FRONTS, send, 0)

        @pl.when(front > 0)
        def _():
            def one(index, carry):
                rows = tile(index // 4, 1024)
                columns = tile(lax.rem(index, 4), 512)
                product[rows, columns] = dot(inverse[rows, :], coupling[:, columns]).astype(BF16)
                return carry

            lax.fori_loop(0, 8, one, 0)

        @pl.when(high)
        def _():
            turn(product, turned)

        def one(index, carry):
            rows = tile(index, 512)
            modal_map[rows, :] = dot_last(inverse[rows, :], modes[...]).astype(BF16)
            return carry

        lax.fori_loop(0, NF // 512, one, 0)

    def forward(group):
        rows = tile(group, WIDTH)

        @pl.when(front > group * 2)
        def _():
            copy_fwd(group).wait_recv()

            @pl.when(low)
            def _():
                solved_in[group] = dot(solved_in[group], coupling_turned[...]).astype(BF16)

            result = (0.0 - dot(solved_in[group], turned[...])).astype(BF16)
            first = pl.ds(pl.multiple_of(group * WIDTH, WIDTH), OWN)
            second = pl.ds(pl.multiple_of(group * WIDTH + OWN, OWN), OWN)
            solved[first, :] = result[:OWN]

            @pl.when(front > group * 2 + 1)
            def _():
                solved[second, :] = result[OWN:]

        @pl.when(front < FRONTS - 1)
        def _():
            copy_fwd(group).start()

    def backward(group):
        rows = tile(group, WIDTH)

        @pl.when(front < FRONTS - 1)
        def _():
            copy_bwd(group).wait_recv()
            back[rows, :] = (solved[rows, :].astype(F32) - handed_in[group].astype(F32)).astype(BF16)

        @pl.when(front == FRONTS - 1)
        def _():
            back[rows, :] = solved[rows, :]

        @pl.when(front > 0)
        def _():
            handed[group] = dot(back[rows, :], product[...]).astype(BF16)
            copy_bwd(group).start()

        modal_out[group] = dot(back[rows, :], modal_map[...])

        @pl.when(front < FRONTS - 1)
        def _():
            copy_sum(group).wait_recv()
            modal_out[group] = modal_out[group] + modal_in[group]

        @pl.when(front > 0)
        def _():
            copy_sum(group).start()

        @pl.when(front == 0)
        def _():
            modal[rows, :] = modal_out[group].astype(BF16)

            def send(step, carry):
                copy_modal(group, step).start()
                return carry

            lax.fori_loop(1, FRONTS, send, 0)

    map_slot = jnp.where(high, 0, front + 1)

    def slot(moment, carry):
        @pl.when(moment == map_slot)
        def _():
            build_maps()

        ahead = front - moment
        behind = 15 - front - moment

        @pl.when(jnp.logical_and(ahead >= 0, lax.rem(ahead + 16, 2) == 0))
        def _():
            forward(ahead // 2)

        @pl.when(
            jnp.logical_and(
                jnp.logical_and(behind >= 0, behind < 2 * GROUPS), lax.rem(behind + 16, 2) == 0
            )
        )
        def _():
            backward(behind // 2)

        return carry

    lax.fori_loop(0, 16, slot, 0)

    entries[own_rows, :] = dot_last(own[...], back[...])

    def send_entry(step, carry):
        copy_entry(step, front).start()
        return carry

    lax.fori_loop(1, FRONTS, send_entry, 0)

    def displace(index, carry):
        columns = tile(index, 512)
        displaced[:, columns] = dot(back[...], inverse[:, columns])
        return carry

    lax.fori_loop(0, NF // 512, displace, 0)

    @pl.when(front > 0)
    def _():
        def wait(group, carry):
            copy_modal(group, 1).wait_recv()
            return carry

        lax.fori_loop(0, GROUPS, wait, 0)

    def wait_rows(step, carry):
        copy_mode(step, peer_front(step)).wait_recv()
        copy_entry(step, peer_front(step)).wait_recv()
        return carry

    lax.fori_loop(1, FRONTS, wait_rows, 0)
    flexible = (entries[...] - dot_last(mode_rows[...], modal[...])).astype(BF16)
    routed = dot(route[...], flexible).astype(BF16)
    rows_out[...] = routed.reshape(SUBS, SHARE, COLS)

    def send_row(step, carry):
        copy_row(step, sub).start()
        return carry

    lax.fori_loop(1, SUBS, send_row, 0)
    rows_in[sub] = rows_out[sub]

    def deflate(index, carry):
        columns = tile(index, 512)
        attachment[:, columns] = (displaced[:, columns] - dot(modal[...], modes[:, columns])).astype(BF16)
        return carry

    lax.fori_loop(0, NF // 512, deflate, 0)
    store = pltpu.make_async_copy(attachment, attachment_hbm.at[0], store_sem.at[0])
    store.start()

    def wait_row(step, carry):
        copy_row(step, peer_sub(step)).wait_recv()
        return carry

    lax.fori_loop(1, SUBS, wait_row, 0)
    high_place = lax.broadcasted_iota(jnp.int32, (SUBS, SHARE, COLS), 0)

    def spread(index, total):
        level = lax.shift_right_logical(ids_ref[pl.ds(index, 1), :], 7)
        chosen = jnp.where(
            high_place == level[:, None, :], rows_in[index].astype(F32)[None, :, :], 0.0
        ).astype(BF16)
        return total + dot_last(chosen.reshape(SUBS * SHARE, COLS), low_pick[index])

    total = lax.fori_loop(0, SUBS, spread, jnp.zeros((SUBS * SHARE, 128), F32))
    for index in range(SUBS):
        flexibility[:, index * 128 : (index + 1) * 128] = total[index * SHARE : (index + 1) * SHARE]
    store_flexibility = pltpu.make_async_copy(flexibility, flexibility_hbm, store_sem.at[1])
    store_flexibility.start()

    @pl.when(front < FRONTS - 1)
    def _():
        def wait(group, carry):
            copy_fwd(group).wait_send()
            return carry

        lax.fori_loop(0, front // 2 + 1, wait, 0)

    @pl.when(front > 0)
    def _():
        def wait(group, carry):
            copy_bwd(group).wait_send()
            copy_sum(group).wait_send()
            return carry

        lax.fori_loop(0, GROUPS, wait, 0)

    @pl.when(front == 0)
    def _():
        def wait(index, carry):
            copy_modal(index // 7, lax.rem(index, 7) + 1).wait_send()
            return carry

        lax.fori_loop(0, GROUPS * 7, wait, 0)

    def wait_sends(step, carry):
        copy_mode(step, front).wait_send()
        copy_entry(step, front).wait_send()
        return carry

    lax.fori_loop(1, FRONTS, wait_sends, 0)

    def wait_row_sends(step, carry):
        copy_row(step, sub).wait_send()
        return carry

    lax.fori_loop(1, SUBS, wait_row_sends, 0)
    store.wait()
    store_flexibility.wait()


def on_device(front_inverse, coupling, free_modes, dof_offset, interface_id):
    dma = pltpu.SemaphoreType.DMA
    vmem = pltpu.VMEM
    anywhere = pl.BlockSpec(memory_space=pl.ANY)
    local = pl.BlockSpec(memory_space=pltpu.VMEM)
    return pl.pallas_call(
        kernel,
        out_shape=(
            jax.ShapeDtypeStruct((1, COLS, NF), BF16),
            jax.ShapeDtypeStruct((SHARE, NF), F32),
        ),
        in_specs=[anywhere, anywhere, anywhere, local, local],
        out_specs=(anywhere, anywhere),
        scratch_shapes=[
            vmem((NF, NF), BF16),
            vmem((NF, NF), BF16),
            vmem((MODES, NF), BF16),
            vmem((MPAD, NF), BF16),
            vmem((NF, NF), BF16),
            vmem((NF, NF), BF16),
            vmem((NF, NF), BF16),
            vmem((NF, MPAD), BF16),
            vmem((OWN, NF), BF16),
            vmem((OWN, NF), BF16),
            vmem((COLS, NF), BF16),
            vmem((GROUPS, WIDTH, NF), BF16),
            vmem((COLS, NF), BF16),
            vmem((GROUPS, WIDTH, NF), BF16),
            vmem((GROUPS, WIDTH, NF), BF16),
            vmem((GROUPS, WIDTH, MPAD), F32),
            vmem((GROUPS, WIDTH, MPAD), F32),
            vmem((COLS, MPAD), BF16),
            vmem((COLS, MPAD), BF16),
            vmem((COLS, COLS), F32),
            vmem((COLS, COLS), BF16),
            vmem((SUBS, SHARE, COLS), BF16),
            vmem((SUBS, SHARE, COLS), BF16),
            vmem((SUBS, 128, COLS), BF16),
            vmem((COLS, NF), F32),
            vmem((COLS, NF), BF16),
            vmem((SHARE, NF), F32),
            dma((3,)),
            dma((GROUPS,)),
            dma((GROUPS,)),
            dma((GROUPS,)),
            dma((GROUPS,)),
            dma((GROUPS,)),
            dma((GROUPS,)),
            dma((GROUPS, FRONTS)),
            dma((GROUPS,)),
            dma((FRONTS,)),
            dma((FRONTS,)),
            dma((FRONTS,)),
            dma((FRONTS,)),
            dma((SUBS,)),
            dma((SUBS,)),
            dma((2,)),
        ],
        compiler_params=pltpu.CompilerParams(
            collective_id=0, has_side_effects=True, vmem_limit_bytes=60 << 20
        ),
        name="chain",
    )(front_inverse, coupling, free_modes, dof_offset, interface_id)


def solution(mesh):
    return jax.shard_map(
        on_device,
        mesh=mesh,
        in_specs=(
            P("sub", "front", None),
            P("sub", "front", None),
            P("sub", None, "front"),
            P("sub", "front"),
            P(),
        ),
        out_specs=(P("sub", None, "front"), P(("sub", "front"), None)),
        check_vma=False,
    )
```

```python
import functools

import jax
import jax.numpy as jnp
from jax import lax
from jax.experimental import pallas as pl
from jax.experimental.pallas import tpu as pltpu
from jax.sharding import PartitionSpec as P

MESH = pl.DeviceIdType.MESH
F32 = jnp.float32
BF16 = jnp.bfloat16

FRONTS = 8
SUBS = 16
NF = 2048
COLS = 256
OWN = 32
GROUPS = 5
WIDTH = 64
VROWS = GROUPS * WIDTH
CHUNK = 512
CHUNKS = NF // CHUNK
MODES = 300
MPAD = 384
SHARE = 16
HIGH = 4
HALF = COLS // 2


def dot(left, right):
    return jnp.dot(left, right, preferred_element_type=F32)


def dot_last(left, right):
    return lax.dot_general(left, right, (((1,), (1,)), ((), ())), preferred_element_type=F32)


def tile(index, size):
    return pl.ds(pl.multiple_of(index * size, size), size)


def kernel(
    inverse_hbm,
    coupling_hbm,
    modes_hbm,
    offsets_ref,
    ids_ref,
    attachment_hbm,
    flexibility_hbm,
    inverse,
    coupling,
    modes_raw,
    modes,
    turned,
    coupling_turned,
    modal_map,
    pick,
    own,
    solved,
    solved_in,
    reduced,
    back,
    handed,
    handed_in,
    modal_out,
    modal_in,
    modal,
    mode_rows,
    entries,
    route,
    rows_out,
    rows_in,
    low_pick,
    displaced,
    attachment,
    flexibility,
    inverse_sem,
    coupling_sem,
    modes_sem,
    fwd_send,
    fwd_recv,
    bwd_send,
    bwd_recv,
    sum_send,
    sum_recv,
    modal_send,
    modal_recv,
    mode_send,
    mode_recv,
    entry_send,
    entry_recv,
    row_send,
    row_recv,
    store_sem,
):
    front = lax.axis_index("front")
    sub = lax.axis_index("sub")
    subs = lax.axis_size("sub")
    last = FRONTS - 1
    high = front >= HIGH
    low = front < HIGH

    def chunk(index):
        return tile(index, CHUNK)

    def load_inverse(index):
        rows = chunk(index)
        return pltpu.make_async_copy(inverse_hbm.at[0, rows], inverse.at[rows], inverse_sem.at[index])

    def load_coupling(index):
        rows = chunk(index)
        return pltpu.make_async_copy(coupling_hbm.at[0, rows], coupling.at[rows], coupling_sem.at[index])

    load_modes = pltpu.make_async_copy(modes_hbm.at[0], modes_raw, modes_sem)
    for index in range(CHUNKS):
        load_inverse(index).start()
    for index in range(CHUNKS):
        load_coupling(index).start()
    load_modes.start()

    def peer_front(step):
        return lax.rem(front + step, FRONTS)

    def peer_sub(step):
        return lax.rem(sub + step, subs)

    barrier = pltpu.get_barrier_semaphore()

    def greet_front(step, carry):
        pl.semaphore_signal(barrier, inc=1, device_id={"front": peer_front(step)}, device_id_type=MESH)
        return carry

    def greet_sub(step, carry):
        pl.semaphore_signal(barrier, inc=1, device_id={"sub": peer_sub(step)}, device_id_type=MESH)
        return carry

    lax.fori_loop(1, FRONTS, greet_front, 0)
    lax.fori_loop(1, subs, greet_sub, 0)

    offsets_square = jnp.broadcast_to(offsets_ref[...].astype(F32), (OWN, OWN))
    diagonal = lax.broadcasted_iota(jnp.int32, (OWN, OWN), 0) == lax.broadcasted_iota(
        jnp.int32, (OWN, OWN), 1
    )
    offsets_column = jnp.sum(
        jnp.where(diagonal, offsets_square, 0.0), axis=1, keepdims=True
    ).astype(jnp.int32)
    pick[...] = (offsets_column == lax.broadcasted_iota(jnp.int32, (OWN, NF), 1)).astype(F32).astype(BF16)
    solved[...] = jnp.zeros((VROWS, NF), BF16)
    solved_in[0, :OWN] = jnp.zeros((OWN, NF), BF16)
    handed_in[0, :OWN] = jnp.zeros((OWN, NF), BF16)
    modal_in[0, :OWN] = jnp.zeros((OWN, MPAD), F32)

    @pl.when(front == 0)
    def _():
        def one(index, carry):
            load_inverse(index).wait()
            own[:, chunk(index)] = dot_last(pick[...], inverse[chunk(index), :]).astype(BF16)
            return carry

        lax.fori_loop(0, CHUNKS, one, 0)

    @pl.when(front > 0)
    def _():
        def one(index, carry):
            load_inverse(index).wait()
            block = inverse[chunk(index), :].T
            turned[:, chunk(index)] = block
            own[:, chunk(index)] = dot(pick[...], block).astype(BF16)
            return carry

        lax.fori_loop(0, CHUNKS, one, 0)

    own_virtual = pl.ds(pl.multiple_of(front * OWN + OWN, OWN), OWN)
    solved[own_virtual, :] = own[...]
    pl.semaphore_wait(barrier, FRONTS - 1 + subs - 1)

    def rows_of(group):
        return tile(group, WIDTH)

    def second_of(group):
        return pl.ds(pl.multiple_of(group * WIDTH + OWN, OWN), OWN)

    after = jnp.minimum(front + 1, last)
    before = jnp.maximum(front - 1, 0)
    whole = pl.ds(0, NF)

    def copy_fwd(group, small, columns):
        inner = pl.ds(OWN, OWN) if small else pl.ds(0, WIDTH)
        return pltpu.make_async_remote_copy(
            src_ref=solved.at[second_of(group) if small else rows_of(group), columns],
            dst_ref=solved_in.at[group, inner, columns],
            send_sem=fwd_send.at[group],
            recv_sem=fwd_recv.at[group],
            device_id={"front": after},
            device_id_type=MESH,
        )

    def copy_bwd(group, small, columns):
        inner = pl.ds(OWN, OWN) if small else pl.ds(0, WIDTH)
        return pltpu.make_async_remote_copy(
            src_ref=handed.at[group, inner, columns],
            dst_ref=handed_in.at[group, inner, columns],
            send_sem=bwd_send.at[group],
            recv_sem=bwd_recv.at[group],
            device_id={"front": before},
            device_id_type=MESH,
        )

    def copy_sum(group, small):
        inner = pl.ds(OWN, OWN) if small else pl.ds(0, WIDTH)
        return pltpu.make_async_remote_copy(
            src_ref=modal_out.at[group, inner],
            dst_ref=modal_in.at[group, inner],
            send_sem=sum_send.at[group],
            recv_sem=sum_recv.at[group],
            device_id={"front": before},
            device_id_type=MESH,
        )

    def copy_modal(group, small, step):
        rows = second_of(group) if small else rows_of(group)
        return pltpu.make_async_remote_copy(
            src_ref=modal.at[rows],
            dst_ref=modal.at[rows],
            send_sem=modal_send.at[group, step],
            recv_sem=modal_recv.at[group],
            device_id={"front": peer_front(step)},
            device_id_type=MESH,
        )

    def by_size(group, act):
        @pl.when(group == 0)
        def _():
            act(True)

        @pl.when(group > 0)
        def _():
            act(False)

    def own_part(index):
        return pl.ds(pl.multiple_of(index * OWN, OWN), OWN)

    def copy_mode(step, index):
        rows = own_part(index)
        return pltpu.make_async_remote_copy(
            src_ref=mode_rows.at[rows],
            dst_ref=mode_rows.at[rows],
            send_sem=mode_send.at[step],
            recv_sem=mode_recv.at[index],
            device_id={"front": peer_front(step)},
            device_id_type=MESH,
        )

    def copy_entry(half, step, index):
        rows = own_part(index)
        return pltpu.make_async_remote_copy(
            src_ref=entries.at[half, rows],
            dst_ref=entries.at[half, rows],
            send_sem=entry_send.at[half, step],
            recv_sem=entry_recv.at[half, index],
            device_id={"front": peer_front(step)},
            device_id_type=MESH,
        )

    def copy_row(step, source):
        return pltpu.make_async_remote_copy(
            src_ref=rows_out.at[peer_sub(step)],
            dst_ref=rows_in.at[source],
            send_sem=row_send.at[step],
            recv_sem=row_recv.at[source],
            device_id={"sub": peer_sub(step)},
            device_id_type=MESH,
        )

    @pl.when(front == 0)
    def _():
        copy_fwd(0, True, whole).start()

    @pl.when(front > 0)
    def _():
        def one(index, carry):
            load_coupling(index).wait()
            coupling_turned[:, chunk(index)] = coupling[chunk(index), :].T
            return carry

        lax.fori_loop(0, CHUNKS, one, 0)

    @pl.when(front == 0)
    def _():
        def one(index, carry):
            load_coupling(index).wait()
            return carry

        lax.fori_loop(0, CHUNKS, one, 0)

    def build_maps():
        load_modes.wait()
        modes[...] = jnp.zeros((MPAD, NF), BF16)
        modes[pl.ds(0, MODES), :] = modes_raw[...]
        mode_rows[own_part(front), :] = dot_last(pick[...], modes[...]).astype(BF16)

        def send(step, carry):
            copy_mode(step, front).start()
            return carry

        lax.fori_loop(1, FRONTS, send, 0)

        place = lax.broadcasted_iota(jnp.int32, (COLS, COLS), 0)
        target = (
            lax.shift_right_logical(place, 4) * (FRONTS * SHARE)
            + jnp.bitwise_and(place, 15)
            + front * SHARE
        )
        route[...] = (target == ids_ref[pl.ds(sub, 1), :]).astype(F32).astype(BF16)
        lane_place = lax.broadcasted_iota(jnp.int32, (128, COLS), 0)

        def fill_low(index, carry):
            ids = jnp.bitwise_and(ids_ref[pl.ds(index, 1), :], 127)
            low_pick[index] = (lane_place == ids).astype(F32).astype(BF16)
            return carry

        lax.fori_loop(0, SUBS, fill_low, 0)

        @pl.when(jnp.logical_and(low, front > 0))
        def _():
            def one(index, carry):
                rows = tile(index // 4, 1024)
                columns = chunk(lax.rem(index, 4))
                turned[rows, columns] = dot(inverse[rows, :], coupling[:, columns]).astype(BF16)
                return carry

            lax.fori_loop(0, 8, one, 0)

        @pl.when(low)
        def _():
            def one(index, carry):
                rows = chunk(index)
                modal_map[rows, :] = dot_last(inverse[rows, :], modes[...]).astype(BF16)
                return carry

            lax.fori_loop(0, CHUNKS, one, 0)

    def forward(group):
        arrives = front >= jnp.maximum(2 * group, 1)

        @pl.when(arrives)
        def _():
            by_size(group, lambda small: copy_fwd(group, small, whole).wait_recv())
            reduced[...] = dot(solved_in[group], coupling_turned[...]).astype(BF16)
            for index in range(CHUNKS):
                columns = pl.ds(index * CHUNK, CHUNK)
                result = (0.0 - dot(reduced[...], turned[:, columns])).astype(BF16)
                solved[tile(group * 2, OWN), columns] = result[:OWN]

                @pl.when(front > group * 2)
                def _():
                    solved[second_of(group), columns] = result[OWN:]

                @pl.when(front < last)
                def _():
                    by_size(group, lambda small: copy_fwd(group, small, columns).start())

        @pl.when(jnp.logical_and(front < last, front == 2 * group - 1))
        def _():
            copy_fwd(group, False, whole).start()

    def send_entries(half):
        columns = pl.ds(OWN + half * HALF, HALF)
        entries[half, own_part(front)] = dot_last(own[...], back[columns, :])
        for step in (4, 5, 3, 2, 6, 7, 1):
            copy_entry(half, step, front).start()

    def backward(group):
        rows = rows_of(group)

        @pl.when(front < last)
        def _():
            by_size(group, lambda small: copy_bwd(group, small, whole).wait_recv())
            back[rows, :] = (solved[rows, :].astype(F32) - handed_in[group].astype(F32)).astype(BF16)

        @pl.when(front == last)
        def _():
            back[rows, :] = solved[rows, :]

        @pl.when(low)
        def _():
            @pl.when(front > 0)
            def _():
                for index in range(CHUNKS):
                    columns = pl.ds(index * CHUNK, CHUNK)
                    handed[group, :, columns] = dot(back[rows, :], turned[:, columns]).astype(BF16)
                    by_size(group, lambda small: copy_bwd(group, small, columns).start())

            modal_out[group] = dot(back[rows, :], modal_map[...])

        @pl.when(high)
        def _():
            moved = dot(back[rows, :], inverse[...])
            displaced[rows, :] = moved
            reduced[...] = moved.astype(BF16)
            for index in range(CHUNKS):
                columns = pl.ds(index * CHUNK, CHUNK)
                handed[group, :, columns] = dot(reduced[...], coupling[:, columns]).astype(BF16)
                by_size(group, lambda small: copy_bwd(group, small, columns).start())
            modal_out[group] = dot_last(reduced[...], modes[...])

        @pl.when(front < last)
        def _():
            by_size(group, lambda small: copy_sum(group, small).wait_recv())
            modal_out[group] = modal_out[group] + modal_in[group]

        @pl.when(front > 0)
        def _():
            by_size(group, lambda small: copy_sum(group, small).start())

        @pl.when(front == 0)
        def _():
            modal[rows, :] = modal_out[group].astype(BF16)

            def send(small):
                for step in (4, 5, 3, 2, 6, 7, 1):
                    copy_modal(group, small, step).start()

            by_size(group, send)

        @pl.when(group == 1)
        def _():
            send_entries(1)

    map_slot = jnp.where(high, 0, front + 2)

    def slot(moment, carry):
        @pl.when(moment == map_slot)
        def _():
            build_maps()

        ahead = front + 1 - moment
        behind = 16 - front - moment

        @pl.when(jnp.logical_and(ahead >= 0, lax.rem(ahead + 16, 2) == 0))
        def _():
            forward(ahead // 2)

        @pl.when(
            jnp.logical_and(
                jnp.logical_and(behind >= 0, behind < 2 * GROUPS), lax.rem(behind + 16, 2) == 0
            )
        )
        def _():
            backward(behind // 2)

        return carry

    lax.fori_loop(0, 17, slot, 0)
    send_entries(0)
    real = pl.ds(OWN, COLS)

    @pl.when(low)
    def _():
        def displace(index, carry):
            columns = chunk(index)
            displaced[real, columns] = dot(back[real, :], inverse[:, columns])
            return carry

        lax.fori_loop(0, CHUNKS, displace, 0)

    @pl.when(front > 0)
    def _():
        def wait(group, carry):
            copy_modal(group, False, 1).wait_recv()
            return carry

        lax.fori_loop(1, GROUPS, wait, 0)
        copy_modal(0, True, 1).wait_recv()

    def wait_rows(step, carry):
        copy_mode(step, peer_front(step)).wait_recv()
        copy_entry(0, step, peer_front(step)).wait_recv()
        copy_entry(1, step, peer_front(step)).wait_recv()
        return carry

    lax.fori_loop(1, FRONTS, wait_rows, 0)
    projected = dot_last(mode_rows[...], modal[real, :])
    for half in range(2):
        lanes = slice(half * HALF, (half + 1) * HALF)
        flexible = (entries[half] - projected[:, lanes]).astype(BF16)
        rows_out[:, :, lanes] = dot(route[...], flexible).astype(BF16).reshape(SUBS, SHARE, HALF)

    def send_row(step, carry):
        copy_row(step, sub).start()
        return carry

    lax.fori_loop(1, subs, send_row, 0)
    rows_in[sub] = rows_out[sub]

    def deflate(index, carry):
        columns = chunk(index)
        attachment[:, columns] = (
            displaced[real, columns] - dot(modal[real, :], modes[:, columns])
        ).astype(BF16)
        return carry

    lax.fori_loop(0, CHUNKS, deflate, 0)
    store = pltpu.make_async_copy(attachment, attachment_hbm.at[0], store_sem.at[0])
    store.start()

    def wait_row(step, carry):
        copy_row(step, peer_sub(step)).wait_recv()
        return carry

    lax.fori_loop(1, subs, wait_row, 0)
    high_place = lax.broadcasted_iota(jnp.int32, (SUBS, SHARE, COLS), 0)

    def spread(index, total):
        level = lax.shift_right_logical(ids_ref[pl.ds(index, 1), :], 7)
        chosen = jnp.where(
            high_place == level[:, None, :], rows_in[index].astype(F32)[None, :, :], 0.0
        ).astype(BF16)
        return total + dot_last(chosen.reshape(SUBS * SHARE, COLS), low_pick[index])

    total = lax.fori_loop(0, SUBS, spread, jnp.zeros((SUBS * SHARE, 128), F32))
    for index in range(SUBS):
        flexibility[:, index * 128 : (index + 1) * 128] = total[index * SHARE : (index + 1) * SHARE]
    store_flexibility = pltpu.make_async_copy(flexibility, flexibility_hbm, store_sem.at[1])
    store_flexibility.start()

    @pl.when(front < last)
    def _():
        copy_fwd(0, True, whole).wait_send()

        def wait(group, carry):
            copy_fwd(group, False, whole).wait_send()
            return carry

        lax.fori_loop(1, (front + 1) // 2 + 1, wait, 0)

    @pl.when(front > 0)
    def _():
        copy_bwd(0, True, whole).wait_send()
        copy_sum(0, True).wait_send()

        def wait(group, carry):
            copy_bwd(group, False, whole).wait_send()
            copy_sum(group, False).wait_send()
            return carry

        lax.fori_loop(1, GROUPS, wait, 0)

    @pl.when(front == 0)
    def _():
        def wait(index, carry):
            copy_modal(index // 7, False, lax.rem(index, 7) + 1).wait_send()
            return carry

        lax.fori_loop(7, GROUPS * 7, wait, 0)

        def wait_small(index, carry):
            copy_modal(0, True, index).wait_send()
            return carry

        lax.fori_loop(1, FRONTS, wait_small, 0)

    def wait_sends(step, carry):
        copy_mode(step, front).wait_send()
        copy_entry(0, step, front).wait_send()
        copy_entry(1, step, front).wait_send()
        return carry

    lax.fori_loop(1, FRONTS, wait_sends, 0)

    def wait_row_sends(step, carry):
        copy_row(step, sub).wait_send()
        return carry

    lax.fori_loop(1, subs, wait_row_sends, 0)
    store.wait()
    store_flexibility.wait()


def on_device(front_inverse, coupling, free_modes, dof_offset, interface_id):
    dma = pltpu.SemaphoreType.DMA
    vmem = pltpu.VMEM
    anywhere = pl.BlockSpec(memory_space=pl.ANY)
    local = pl.BlockSpec(memory_space=pltpu.VMEM)
    return pl.pallas_call(
        kernel,
        out_shape=(
            jax.ShapeDtypeStruct((1, COLS, NF), BF16),
            jax.ShapeDtypeStruct((SHARE, NF), F32),
        ),
        in_specs=[anywhere, anywhere, anywhere, local, local],
        out_specs=(anywhere, anywhere),
        scratch_shapes=[
            vmem((NF, NF), BF16),
            vmem((NF, NF), BF16),
            vmem((MODES, NF), BF16),
            vmem((MPAD, NF), BF16),
            vmem((NF, NF), BF16),
            vmem((NF, NF), BF16),
            vmem((NF, MPAD), BF16),
            vmem((OWN, NF), BF16),
            vmem((OWN, NF), BF16),
            vmem((VROWS, NF), BF16),
            vmem((GROUPS, WIDTH, NF), BF16),
            vmem((WIDTH, NF), BF16),
            vmem((VROWS, NF), BF16),
            vmem((GROUPS, WIDTH, NF), BF16),
            vmem((GROUPS, WIDTH, NF), BF16),
            vmem((GROUPS, WIDTH, MPAD), F32),
            vmem((GROUPS, WIDTH, MPAD), F32),
            vmem((VROWS, MPAD), BF16),
            vmem((COLS, MPAD), BF16),
            vmem((2, COLS, HALF), F32),
            vmem((COLS, COLS), BF16),
            vmem((SUBS, SHARE, COLS), BF16),
            vmem((SUBS, SHARE, COLS), BF16),
            vmem((SUBS, 128, COLS), BF16),
            vmem((VROWS, NF), F32),
            vmem((COLS, NF), BF16),
            vmem((SHARE, NF), F32),
            dma((CHUNKS,)),
            dma((CHUNKS,)),
            dma,
            dma((GROUPS,)),
            dma((GROUPS,)),
            dma((GROUPS,)),
            dma((GROUPS,)),
            dma((GROUPS,)),
            dma((GROUPS,)),
            dma((GROUPS, FRONTS)),
            dma((GROUPS,)),
            dma((FRONTS,)),
            dma((FRONTS,)),
            dma((2, FRONTS)),
            dma((2, FRONTS)),
            dma((SUBS,)),
            dma((SUBS,)),
            dma((2,)),
        ],
        compiler_params=pltpu.CompilerParams(
            collective_id=0, has_side_effects=True, vmem_limit_bytes=60 << 20
        ),
        name="chain",
    )(front_inverse, coupling, free_modes, dof_offset, interface_id)


def solution(mesh):
    return jax.shard_map(
        on_device,
        mesh=mesh,
        in_specs=(
            P("sub", "front", None),
            P("sub", "front", None),
            P("sub", None, "front"),
            P("sub", "front"),
            P(),
        ),
        out_specs=(P("sub", None, "front"), P(("sub", "front"), None)),
        check_vma=False,
    )
```

```python
import functools

import jax
import jax.numpy as jnp
from jax import lax
from jax.experimental import pallas as pl
from jax.experimental.pallas import tpu as pltpu
from jax.sharding import PartitionSpec as P

MESH = pl.DeviceIdType.MESH
F32 = jnp.float32
BF16 = jnp.bfloat16

FRONTS = 8
SUBS = 16
NF = 2048
COLS = 256
OWN = 32
STARTS = (0, 1, 3, 5, 8)
GROUPS = len(STARTS) - 1
CHUNK = 512
CHUNKS = NF // CHUNK
MODES = 300
MPAD = 384
SHARE = 16
HALF = COLS // 2


def dot(left, right):
    return jnp.dot(left, right, preferred_element_type=F32)


def dot_last(left, right):
    return lax.dot_general(left, right, (((1,), (1,)), ((), ())), preferred_element_type=F32)


def dot_wide(left, right):
    count = left.shape[0]
    if count < 128:
        left = jnp.concatenate([left, left, left, left][: 128 // count] + [left[: 128 % count]] * (128 % count > 0), axis=0)
    return dot(left, right)[:count]


def tile(index, size):
    return pl.ds(pl.multiple_of(index * size, size), size)


def kernel(
    inverse_hbm,
    coupling_hbm,
    modes_hbm,
    offsets_ref,
    ids_ref,
    attachment_hbm,
    flexibility_hbm,
    inverse,
    coupling,
    modes_raw,
    modes,
    turned,
    coupling_turned,
    modal_map,
    gathered,
    pick,
    own,
    solved,
    solved_in,
    reduced,
    back,
    handed,
    handed_in,
    modal_out,
    modal_in,
    modal,
    mode_rows,
    entries,
    route,
    rows_out,
    rows_in,
    low_pick,
    displaced,
    attachment,
    flexibility,
    inverse_sem,
    coupling_sem,
    modes_sem,
    fwd_send,
    fwd_recv,
    bwd_send,
    bwd_recv,
    sum_send,
    sum_recv,
    modal_send,
    modal_recv,
    mode_send,
    mode_recv,
    entry_send,
    entry_recv,
    row_send,
    row_recv,
    store_sem,
):
    front = lax.axis_index("front")
    sub = lax.axis_index("sub")
    subs = lax.axis_size("sub")
    last = FRONTS - 1

    def chunk(index):
        return tile(index, CHUNK)

    def load_inverse(index):
        rows = chunk(index)
        return pltpu.make_async_copy(inverse_hbm.at[0, rows], inverse.at[rows], inverse_sem.at[index])

    def load_coupling(index):
        rows = chunk(index)
        return pltpu.make_async_copy(coupling_hbm.at[0, rows], coupling.at[rows], coupling_sem.at[index])

    load_modes = pltpu.make_async_copy(modes_hbm.at[0], modes_raw, modes_sem)
    for index in range(CHUNKS):
        load_inverse(index).start()
    for index in range(CHUNKS):
        load_coupling(index).start()
    load_modes.start()

    def peer_front(step):
        return lax.rem(front + step, FRONTS)

    def peer_sub(step):
        return lax.rem(sub + step, subs)

    barrier = pltpu.get_barrier_semaphore()

    def greet_front(step, carry):
        pl.semaphore_signal(barrier, inc=1, device_id={"front": peer_front(step)}, device_id_type=MESH)
        return carry

    def greet_sub(step, carry):
        pl.semaphore_signal(barrier, inc=1, device_id={"sub": peer_sub(step)}, device_id_type=MESH)
        return carry

    lax.fori_loop(1, FRONTS, greet_front, 0)
    lax.fori_loop(1, subs, greet_sub, 0)

    offsets_square = jnp.broadcast_to(offsets_ref[...].astype(F32), (OWN, OWN))
    diagonal = lax.broadcasted_iota(jnp.int32, (OWN, OWN), 0) == lax.broadcasted_iota(
        jnp.int32, (OWN, OWN), 1
    )
    offsets_column = jnp.sum(
        jnp.where(diagonal, offsets_square, 0.0), axis=1, keepdims=True
    ).astype(jnp.int32)
    pick[...] = (offsets_column == lax.broadcasted_iota(jnp.int32, (OWN, NF), 1)).astype(F32).astype(BF16)
    solved[...] = jnp.zeros((COLS, NF), BF16)

    @pl.when(front == 0)
    def _():
        def one(index, carry):
            load_inverse(index).wait()
            own[:, chunk(index)] = dot_last(pick[...], inverse[chunk(index), :]).astype(BF16)
            return carry

        lax.fori_loop(0, CHUNKS, one, 0)

    @pl.when(front > 0)
    def _():
        def one(index, carry):
            load_inverse(index).wait()
            block = inverse[chunk(index), :].T
            turned[:, chunk(index)] = block
            own[:, chunk(index)] = dot(pick[...], block).astype(BF16)
            return carry

        lax.fori_loop(0, CHUNKS, one, 0)

    own_rows = pl.ds(pl.multiple_of(front * OWN, OWN), OWN)
    solved[own_rows, :] = own[...]
    pl.semaphore_wait(barrier, FRONTS - 1 + subs - 1)

    def rows_of(group):
        return slice(STARTS[group] * OWN, STARTS[group + 1] * OWN)

    def count_of(group):
        return (STARTS[group + 1] - STARTS[group]) * OWN

    after = jnp.minimum(front + 1, last)
    before = jnp.maximum(front - 1, 0)
    whole = slice(0, NF)

    def chunk_lanes(index):
        return slice(index * CHUNK, (index + 1) * CHUNK)

    def copy_fwd(group, index, columns=None):
        columns = chunk_lanes(index) if columns is None else columns
        return pltpu.make_async_remote_copy(
            src_ref=solved.at[rows_of(group), columns],
            dst_ref=solved_in.at[rows_of(group), columns],
            send_sem=fwd_send.at[group],
            recv_sem=fwd_recv.at[group, index],
            device_id={"front": after},
            device_id_type=MESH,
        )

    def copy_bwd(group, index, columns=None):
        columns = chunk_lanes(index) if columns is None else columns
        return pltpu.make_async_remote_copy(
            src_ref=handed.at[rows_of(group), columns],
            dst_ref=handed_in.at[rows_of(group), columns],
            send_sem=bwd_send.at[group],
            recv_sem=bwd_recv.at[group, index],
            device_id={"front": before},
            device_id_type=MESH,
        )

    def copy_sum(group):
        return pltpu.make_async_remote_copy(
            src_ref=modal_out.at[rows_of(group)],
            dst_ref=modal_in.at[rows_of(group)],
            send_sem=sum_send.at[group],
            recv_sem=sum_recv.at[group],
            device_id={"front": before},
            device_id_type=MESH,
        )

    def copy_modal(group, step):
        return pltpu.make_async_remote_copy(
            src_ref=modal.at[rows_of(group)],
            dst_ref=modal.at[rows_of(group)],
            send_sem=modal_send.at[group, step],
            recv_sem=modal_recv.at[group],
            device_id={"front": peer_front(step)},
            device_id_type=MESH,
        )

    def own_part(index):
        return pl.ds(pl.multiple_of(index * OWN, OWN), OWN)

    def copy_mode(step, index):
        rows = own_part(index)
        return pltpu.make_async_remote_copy(
            src_ref=mode_rows.at[rows],
            dst_ref=mode_rows.at[rows],
            send_sem=mode_send.at[step],
            recv_sem=mode_recv.at[index],
            device_id={"front": peer_front(step)},
            device_id_type=MESH,
        )

    def copy_entry(half, step, index):
        rows = own_part(index)
        return pltpu.make_async_remote_copy(
            src_ref=entries.at[half, rows],
            dst_ref=entries.at[half, rows],
            send_sem=entry_send.at[half, step],
            recv_sem=entry_recv.at[half, index],
            device_id={"front": peer_front(step)},
            device_id_type=MESH,
        )

    def copy_row(step, source):
        return pltpu.make_async_remote_copy(
            src_ref=rows_out.at[peer_sub(step)],
            dst_ref=rows_in.at[source],
            send_sem=row_send.at[step],
            recv_sem=row_recv.at[source],
            device_id={"sub": peer_sub(step)},
            device_id_type=MESH,
        )

    @pl.when(front == 0)
    def _():
        for index in range(CHUNKS):
            copy_fwd(0, index).start()

    @pl.when(front > 1)
    def _():
        def one(index, carry):
            load_coupling(index).wait()
            coupling_turned[:, chunk(index)] = coupling[chunk(index), :].T
            return carry

        lax.fori_loop(0, CHUNKS, one, 0)

    @pl.when(front <= 1)
    def _():
        def one(index, carry):
            load_coupling(index).wait()
            return carry

        lax.fori_loop(0, CHUNKS, one, 0)

    def build_modal_map():
        load_modes.wait()
        modes[...] = jnp.zeros((MPAD, NF), BF16)
        modes[pl.ds(0, MODES), :] = modes_raw[...]

        @pl.when(front == 0)
        def _():
            def one(index, carry):
                rows = chunk(index)
                modal_map[rows, :] = dot_last(inverse[rows, :], modes[...]).astype(BF16)
                return carry

            lax.fori_loop(0, CHUNKS, one, 0)

        @pl.when(front > 0)
        def _():
            def one(index, carry):
                rows = chunk(index)
                modal_map[rows, :] = modes[:, rows].T
                return carry

            lax.fori_loop(0, CHUNKS, one, 0)

    def build_picks():
        mode_rows[own_part(front), :] = dot_last(pick[...], modes[...]).astype(BF16)

        def send(step, carry):
            copy_mode(step, front).start()
            return carry

        lax.fori_loop(1, FRONTS, send, 0)

        place = lax.broadcasted_iota(jnp.int32, (COLS, COLS), 0)
        target = (
            lax.shift_right_logical(place, 4) * (FRONTS * SHARE)
            + jnp.bitwise_and(place, 15)
            + front * SHARE
        )
        route[...] = (target == ids_ref[pl.ds(sub, 1), :]).astype(F32).astype(BF16)
        lane_place = lax.broadcasted_iota(jnp.int32, (128, COLS), 0)

        def fill_low(index, carry):
            ids = jnp.bitwise_and(ids_ref[pl.ds(index, 1), :], 127)
            low_pick[index] = (lane_place == ids).astype(F32).astype(BF16)
            return carry

        lax.fori_loop(0, SUBS, fill_low, 0)

    def forward(group):
        rows = rows_of(group)
        count = count_of(group)
        first = STARTS[group]
        members = STARTS[group + 1] - first

        if group == 0:

            @pl.when(front == 1)
            def _():
                for index in range(CHUNKS):
                    columns = chunk_lanes(index)
                    copy_fwd(group, index).wait_recv()
                    part = dot_last(solved_in[rows, columns], coupling[:, columns])
                    gathered[:count] = part if index == 0 else gathered[:count] + part
                reduced[:count] = gathered[:count].astype(BF16)

        @pl.when(front > max(first, 1))
        def _():
            for index in range(CHUNKS):
                columns = chunk_lanes(index)
                copy_fwd(group, index).wait_recv()
                part = dot_wide(solved_in[rows, columns], coupling_turned[columns, :])
                if index == 0:
                    gathered[:count] = part
                elif index < CHUNKS - 1:
                    gathered[:count] = gathered[:count] + part
                else:
                    reduced[:count] = (gathered[:count] + part).astype(BF16)

        @pl.when(front > first)
        def _():
            for index in range(CHUNKS):
                columns = chunk_lanes(index)
                result = (0.0 - dot_wide(reduced[:count], turned[:, columns])).astype(BF16)
                solved[first * OWN : (first + 1) * OWN, columns] = result[:OWN]
                for member in range(1, members):

                    @pl.when(front > first + member)
                    def _():
                        part = slice(member * OWN, (member + 1) * OWN)
                        solved[(first + member) * OWN : (first + member + 1) * OWN, columns] = result[part]

                @pl.when(front < last)
                def _():
                    copy_fwd(group, index).start()

        if group > 0:

            @pl.when(front == first)
            def _():
                for index in range(CHUNKS):
                    copy_fwd(group, index).start()

    def send_entries(half):
        columns = pl.ds(half * HALF, HALF)
        entries[half, own_part(front)] = dot_last(own[...], back[columns, :])
        for step in (4, 5, 3, 2, 6, 7, 1):
            copy_entry(half, step, front).start()

    def backward(group):
        rows = rows_of(group)
        count = count_of(group)
        for index in range(CHUNKS):
            columns = chunk_lanes(index)

            @pl.when(front < last)
            def _():
                copy_bwd(group, index).wait_recv()
                back[rows, columns] = (
                    solved[rows, columns].astype(F32) - handed_in[rows, columns].astype(F32)
                ).astype(BF16)

            @pl.when(front == last)
            def _():
                back[rows, columns] = solved[rows, columns]

            @pl.when(front > 0)
            def _():
                total = dot_wide(back[rows, columns], inverse[columns, :])
                if index > 0:
                    total = displaced[rows, :] + total
                displaced[rows, :] = total
                if index == CHUNKS - 1:
                    reduced[:count] = total.astype(BF16)

            @pl.when(front == 0)
            def _():
                part = dot_wide(back[rows, columns], modal_map[columns, :])
                modal_out[rows, :] = part if index == 0 else modal_out[rows, :] + part

        @pl.when(front > 0)
        def _():
            for index in range(CHUNKS):
                columns = chunk_lanes(index)
                handed[rows, columns] = dot_wide(reduced[:count], coupling[:, columns]).astype(BF16)
                copy_bwd(group, index).start()

            modal_out[rows, :] = dot_wide(reduced[:count], modal_map[...])

        @pl.when(front < last)
        def _():
            copy_sum(group).wait_recv()
            modal_out[rows, :] = modal_out[rows, :] + modal_in[rows, :]

        @pl.when(front > 0)
        def _():
            copy_sum(group).start()

        @pl.when(front == 0)
        def _():
            modal[rows, :] = modal_out[rows, :].astype(BF16)
            for step in (4, 5, 3, 2, 6, 7, 1):
                copy_modal(group, step).start()
            if group > 0:
                displaced[rows, :] = dot_wide(back[rows, :], inverse[...])

        if group == 2:
            send_entries(1)

    build_modal_at = jnp.where(front < 2, 5, 0)
    build_picks_at = jnp.where(front < 4, 9, 99)

    def slot(moment, carry):
        @pl.when(moment == build_modal_at)
        def _():
            build_modal_map()

        @pl.when(moment == build_picks_at)
        def _():
            build_picks()

        for group in range(GROUPS):
            turn_f = 2 * (front - STARTS[group])
            turn_b = 2 * (15 - STARTS[group] - front) + jnp.where(front >= last - 1, -1, 1)

            @pl.when(moment == turn_f)
            def _():
                forward(group)

            @pl.when(moment == turn_b)
            def _():
                backward(group)

        return carry

    lax.fori_loop(0, 32, slot, 0)
    send_entries(0)

    @pl.when(front >= 4)
    def _():
        build_picks()

    real = slice(0, COLS)

    @pl.when(front > 0)
    def _():
        for group in range(GROUPS):
            copy_modal(group, 1).wait_recv()

    def wait_rows(step, carry):
        copy_mode(step, peer_front(step)).wait_recv()
        copy_entry(0, step, peer_front(step)).wait_recv()
        copy_entry(1, step, peer_front(step)).wait_recv()
        return carry

    lax.fori_loop(1, FRONTS, wait_rows, 0)
    projected = dot_last(mode_rows[...], modal[real, :])
    for half in range(2):
        lanes = slice(half * HALF, (half + 1) * HALF)
        flexible = (entries[half] - projected[:, lanes]).astype(BF16)
        rows_out[:, :, lanes] = dot(route[...], flexible).astype(BF16).reshape(SUBS, SHARE, HALF)

    def send_row(step, carry):
        copy_row(step, sub).start()
        return carry

    lax.fori_loop(1, subs, send_row, 0)
    rows_in[sub] = rows_out[sub]

    @pl.when(front == 0)
    def _():
        rows = rows_of(0)
        displaced[rows, :] = dot_wide(back[rows, :], inverse[...])

    def deflate(index, carry):
        columns = chunk(index)
        attachment[:, columns] = (
            displaced[real, columns] - dot(modal[real, :], modes[:, columns])
        ).astype(BF16)
        return carry

    lax.fori_loop(0, CHUNKS, deflate, 0)
    store = pltpu.make_async_copy(attachment, attachment_hbm.at[0], store_sem.at[0])
    store.start()

    def wait_row(step, carry):
        copy_row(step, peer_sub(step)).wait_recv()
        return carry

    lax.fori_loop(1, subs, wait_row, 0)
    high_place = lax.broadcasted_iota(jnp.int32, (SUBS, SHARE, COLS), 0)

    def spread(index, total):
        level = lax.shift_right_logical(ids_ref[pl.ds(index, 1), :], 7)
        chosen = jnp.where(
            high_place == level[:, None, :], rows_in[index].astype(F32)[None, :, :], 0.0
        ).astype(BF16)
        return total + dot_last(chosen.reshape(SUBS * SHARE, COLS), low_pick[index])

    total = lax.fori_loop(0, SUBS, spread, jnp.zeros((SUBS * SHARE, 128), F32))
    for index in range(SUBS):
        flexibility[:, index * 128 : (index + 1) * 128] = total[index * SHARE : (index + 1) * SHARE]
    store_flexibility = pltpu.make_async_copy(flexibility, flexibility_hbm, store_sem.at[1])
    store_flexibility.start()

    for group in range(GROUPS):

        @pl.when(jnp.logical_and(front < last, front >= STARTS[group]))
        def _():
            copy_fwd(group, 0, whole).wait_send()

        @pl.when(front > 0)
        def _():
            copy_bwd(group, 0, whole).wait_send()
            copy_sum(group).wait_send()

        @pl.when(front == 0)
        def _():
            for step in range(1, FRONTS):
                copy_modal(group, step).wait_send()

    def wait_sends(step, carry):
        copy_mode(step, front).wait_send()
        copy_entry(0, step, front).wait_send()
        copy_entry(1, step, front).wait_send()
        return carry

    lax.fori_loop(1, FRONTS, wait_sends, 0)

    def wait_row_sends(step, carry):
        copy_row(step, sub).wait_send()
        return carry

    lax.fori_loop(1, subs, wait_row_sends, 0)
    store.wait()
    store_flexibility.wait()


def on_device(front_inverse, coupling, free_modes, dof_offset, interface_id):
    dma = pltpu.SemaphoreType.DMA
    vmem = pltpu.VMEM
    anywhere = pl.BlockSpec(memory_space=pl.ANY)
    local = pl.BlockSpec(memory_space=pltpu.VMEM)
    return pl.pallas_call(
        kernel,
        out_shape=(
            jax.ShapeDtypeStruct((1, COLS, NF), BF16),
            jax.ShapeDtypeStruct((SHARE, NF), F32),
        ),
        in_specs=[anywhere, anywhere, anywhere, local, local],
        out_specs=(anywhere, anywhere),
        scratch_shapes=[
            vmem((NF, NF), BF16),
            vmem((NF, NF), BF16),
            vmem((MODES, NF), BF16),
            vmem((MPAD, NF), BF16),
            vmem((NF, NF), BF16),
            vmem((NF, NF), BF16),
            vmem((NF, MPAD), BF16),
            vmem((96, NF), F32),
            vmem((OWN, NF), BF16),
            vmem((OWN, NF), BF16),
            vmem((COLS, NF), BF16),
            vmem((COLS, NF), BF16),
            vmem((96, NF), BF16),
            vmem((COLS, NF), BF16),
            vmem((COLS, NF), BF16),
            vmem((COLS, NF), BF16),
            vmem((COLS, MPAD), F32),
            vmem((COLS, MPAD), F32),
            vmem((COLS, MPAD), BF16),
            vmem((COLS, MPAD), BF16),
            vmem((2, COLS, HALF), F32),
            vmem((COLS, COLS), BF16),
            vmem((SUBS, SHARE, COLS), BF16),
            vmem((SUBS, SHARE, COLS), BF16),
            vmem((SUBS, 128, COLS), BF16),
            vmem((COLS, NF), F32),
            vmem((COLS, NF), BF16),
            vmem((SHARE, NF), F32),
            dma((CHUNKS,)),
            dma((CHUNKS,)),
            dma,
            dma((GROUPS,)),
            dma((GROUPS, CHUNKS)),
            dma((GROUPS,)),
            dma((GROUPS, CHUNKS)),
            dma((GROUPS,)),
            dma((GROUPS,)),
            dma((GROUPS, FRONTS)),
            dma((GROUPS,)),
            dma((FRONTS,)),
            dma((FRONTS,)),
            dma((2, FRONTS)),
            dma((2, FRONTS)),
            dma((SUBS,)),
            dma((SUBS,)),
            dma((2,)),
        ],
        compiler_params=pltpu.CompilerParams(
            collective_id=0, has_side_effects=True, vmem_limit_bytes=60 << 20
        ),
        name="chain",
    )(front_inverse, coupling, free_modes, dof_offset, interface_id)


def solution(mesh):
    return jax.shard_map(
        on_device,
        mesh=mesh,
        in_specs=(
            P("sub", "front", None),
            P("sub", "front", None),
            P("sub", None, "front"),
            P("sub", "front"),
            P(),
        ),
        out_specs=(P("sub", None, "front"), P(("sub", "front"), None)),
        check_vma=False,
    )
```

```python
import functools

import jax
import jax.numpy as jnp
from jax import lax
from jax.experimental import pallas as pl
from jax.experimental.pallas import tpu as pltpu
from jax.sharding import PartitionSpec as P

MESH = pl.DeviceIdType.MESH
F32 = jnp.float32
BF16 = jnp.bfloat16

FRONTS = 8
SUBS = 16
NF = 2048
COLS = 256
OWN = 32
GROUPS = 4
WIDTH = 64
CHUNK = 512
CHUNKS = NF // CHUNK
MODES = 300
MPAD = 384
SHARE = 16
HALF = COLS // 2


def dot(left, right):
    return jnp.dot(left, right, preferred_element_type=F32)


def dot_last(left, right):
    return lax.dot_general(left, right, (((1,), (1,)), ((), ())), preferred_element_type=F32)


def dot_wide(left, right):
    count = left.shape[0]
    if count < 128:
        left = jnp.concatenate([left, left, left, left][: 128 // count] + [left[: 128 % count]] * (128 % count > 0), axis=0)
    return dot(left, right)[:count]


def tile(index, size):
    return pl.ds(pl.multiple_of(index * size, size), size)


def kernel(
    inverse_hbm,
    coupling_hbm,
    modes_hbm,
    offsets_ref,
    ids_ref,
    attachment_hbm,
    flexibility_hbm,
    inverse,
    coupling,
    modes_raw,
    modes,
    turned,
    coupling_turned,
    modal_map,
    gathered,
    pick,
    own,
    solved,
    solved_in,
    reduced,
    back,
    handed,
    handed_in,
    modal_out,
    modal_in,
    modal,
    mode_rows,
    entries,
    route,
    rows_out,
    rows_in,
    low_pick,
    displaced,
    attachment,
    flexibility,
    inverse_sem,
    coupling_sem,
    modes_sem,
    fwd_send,
    fwd_recv,
    bwd_send,
    bwd_recv,
    sum_send,
    sum_recv,
    modal_send,
    modal_recv,
    mode_send,
    mode_recv,
    entry_send,
    entry_recv,
    row_send,
    row_recv,
    store_sem,
):
    front = lax.axis_index("front")
    sub = lax.axis_index("sub")
    subs = lax.axis_size("sub")
    last = FRONTS - 1

    def chunk(index):
        return tile(index, CHUNK)

    def load_inverse(index):
        rows = chunk(index)
        return pltpu.make_async_copy(inverse_hbm.at[0, rows], inverse.at[rows], inverse_sem.at[index])

    def load_coupling(index):
        rows = chunk(index)
        return pltpu.make_async_copy(coupling_hbm.at[0, rows], coupling.at[rows], coupling_sem.at[index])

    load_modes = pltpu.make_async_copy(modes_hbm.at[0], modes_raw, modes_sem)
    for index in range(CHUNKS):
        load_inverse(index).start()

    def peer_front(step):
        return lax.rem(front + step, FRONTS)

    def peer_sub(step):
        return lax.rem(sub + step, subs)

    barrier = pltpu.get_barrier_semaphore()

    def greet_front(step, carry):
        pl.semaphore_signal(barrier, inc=1, device_id={"front": peer_front(step)}, device_id_type=MESH)
        return carry

    def greet_sub(step, carry):
        pl.semaphore_signal(barrier, inc=1, device_id={"sub": peer_sub(step)}, device_id_type=MESH)
        return carry

    lax.fori_loop(1, FRONTS, greet_front, 0)
    lax.fori_loop(1, subs, greet_sub, 0)

    offsets_square = jnp.broadcast_to(offsets_ref[...].astype(F32), (OWN, OWN))
    diagonal = lax.broadcasted_iota(jnp.int32, (OWN, OWN), 0) == lax.broadcasted_iota(
        jnp.int32, (OWN, OWN), 1
    )
    offsets_column = jnp.sum(
        jnp.where(diagonal, offsets_square, 0.0), axis=1, keepdims=True
    ).astype(jnp.int32)
    pick[...] = (offsets_column == lax.broadcasted_iota(jnp.int32, (OWN, NF), 1)).astype(F32).astype(BF16)
    solved[...] = jnp.zeros((COLS, NF), BF16)

    @pl.when(front == 0)
    def _():
        def one(index, carry):
            load_inverse(index).wait()
            load_coupling(index).start()
            own[:, chunk(index)] = dot_last(pick[...], inverse[chunk(index), :]).astype(BF16)
            return carry

        lax.fori_loop(0, CHUNKS, one, 0)

    @pl.when(front > 0)
    def _():
        def one(index, carry):
            load_inverse(index).wait()
            load_coupling(index).start()
            block = inverse[chunk(index), :].T
            turned[:, chunk(index)] = block
            own[:, chunk(index)] = dot(pick[...], block).astype(BF16)
            return carry

        lax.fori_loop(0, CHUNKS, one, 0)

    load_modes.start()
    own_rows = pl.ds(pl.multiple_of(front * OWN, OWN), OWN)
    solved[own_rows, :] = own[...]
    pl.semaphore_wait(barrier, FRONTS - 1 + subs - 1)

    def rows_of(group):
        return tile(group, WIDTH)

    after = jnp.minimum(front + 1, last)
    before = jnp.maximum(front - 1, 0)
    whole = slice(0, NF)

    def chunk_lanes(index):
        return slice(index * CHUNK, (index + 1) * CHUNK)

    def copy_fwd(group, index, columns=None):
        columns = chunk_lanes(index) if columns is None else columns
        return pltpu.make_async_remote_copy(
            src_ref=solved.at[rows_of(group), columns],
            dst_ref=solved_in.at[rows_of(group), columns],
            send_sem=fwd_send.at[group],
            recv_sem=fwd_recv.at[group, index],
            device_id={"front": after},
            device_id_type=MESH,
        )

    def copy_bwd(group, index, columns=None):
        columns = chunk_lanes(index) if columns is None else columns
        return pltpu.make_async_remote_copy(
            src_ref=handed.at[rows_of(group), columns],
            dst_ref=handed_in.at[rows_of(group), columns],
            send_sem=bwd_send.at[group],
            recv_sem=bwd_recv.at[group, index],
            device_id={"front": before},
            device_id_type=MESH,
        )

    def copy_sum(group):
        return pltpu.make_async_remote_copy(
            src_ref=modal_out.at[rows_of(group)],
            dst_ref=modal_in.at[rows_of(group)],
            send_sem=sum_send.at[group],
            recv_sem=sum_recv.at[group],
            device_id={"front": before},
            device_id_type=MESH,
        )

    def copy_modal(group, step):
        return pltpu.make_async_remote_copy(
            src_ref=modal.at[rows_of(group)],
            dst_ref=modal.at[rows_of(group)],
            send_sem=modal_send.at[group, step],
            recv_sem=modal_recv.at[group],
            device_id={"front": peer_front(step)},
            device_id_type=MESH,
        )

    def own_part(index):
        return pl.ds(pl.multiple_of(index * OWN, OWN), OWN)

    def copy_mode(step, index):
        rows = own_part(index)
        return pltpu.make_async_remote_copy(
            src_ref=mode_rows.at[rows],
            dst_ref=mode_rows.at[rows],
            send_sem=mode_send.at[step],
            recv_sem=mode_recv.at[index],
            device_id={"front": peer_front(step)},
            device_id_type=MESH,
        )

    def copy_entry(half, step, index):
        rows = own_part(index)
        return pltpu.make_async_remote_copy(
            src_ref=entries.at[half, rows],
            dst_ref=entries.at[half, rows],
            send_sem=entry_send.at[half, step],
            recv_sem=entry_recv.at[half, index],
            device_id={"front": peer_front(step)},
            device_id_type=MESH,
        )

    def copy_row(step, source):
        return pltpu.make_async_remote_copy(
            src_ref=rows_out.at[peer_sub(step)],
            dst_ref=rows_in.at[source],
            send_sem=row_send.at[step],
            recv_sem=row_recv.at[source],
            device_id={"sub": peer_sub(step)},
            device_id_type=MESH,
        )

    @pl.when(front == 0)
    def _():
        for index in range(CHUNKS):
            copy_fwd(0, index).start()

    @pl.when(front > 0)
    def _():
        def one(index, carry):
            load_coupling(index).wait()
            coupling_turned[:, chunk(index)] = coupling[chunk(index), :].T
            return carry

        lax.fori_loop(0, CHUNKS, one, 0)

    @pl.when(front == 0)
    def _():
        def one(index, carry):
            load_coupling(index).wait()
            return carry

        lax.fori_loop(0, CHUNKS, one, 0)

    def build_modal_map():
        load_modes.wait()
        modes[...] = jnp.zeros((MPAD, NF), BF16)
        modes[pl.ds(0, MODES), :] = modes_raw[...]

        @pl.when(front == 0)
        def _():
            def one(index, carry):
                rows = chunk(index)
                modal_map[rows, :] = dot_last(inverse[rows, :], modes[...]).astype(BF16)
                return carry

            lax.fori_loop(0, CHUNKS, one, 0)

        @pl.when(front > 0)
        def _():
            def one(index, carry):
                rows = chunk(index)
                modal_map[rows, :] = modes[:, rows].T
                return carry

            lax.fori_loop(0, CHUNKS, one, 0)

    def build_picks():
        mode_rows[own_part(front), :] = dot_last(pick[...], modes[...]).astype(BF16)

        def send(step, carry):
            copy_mode(step, front).start()
            return carry

        lax.fori_loop(1, FRONTS, send, 0)

        place = lax.broadcasted_iota(jnp.int32, (COLS, COLS), 0)
        target = (
            lax.shift_right_logical(place, 4) * (FRONTS * SHARE)
            + jnp.bitwise_and(place, 15)
            + front * SHARE
        )
        route[...] = (target == ids_ref[pl.ds(sub, 1), :]).astype(F32).astype(BF16)
        lane_place = lax.broadcasted_iota(jnp.int32, (128, COLS), 0)

        def fill_low(index, carry):
            ids = jnp.bitwise_and(ids_ref[pl.ds(index, 1), :], 127)
            low_pick[index] = (lane_place == ids).astype(F32).astype(BF16)
            return carry

        lax.fori_loop(0, SUBS, fill_low, 0)

    def forward(group):
        rows = rows_of(group)

        @pl.when(front > 2 * group)
        def _():
            for index in range(CHUNKS):
                columns = chunk_lanes(index)
                copy_fwd(group, index).wait_recv()
                part = dot_wide(solved_in[rows, columns], coupling_turned[columns, :])
                if index == 0:
                    gathered[...] = part
                elif index < CHUNKS - 1:
                    gathered[...] = gathered[...] + part
                else:
                    reduced[...] = (gathered[...] + part).astype(BF16)

            first = tile(2 * group, OWN)
            second = tile(2 * group + 1, OWN)
            for index in range(CHUNKS):
                columns = chunk_lanes(index)
                result = 0.0 - dot_wide(reduced[...], turned[:, columns])
                solved[first, columns] = result[:OWN].astype(BF16)
                kept = solved[second, columns].astype(F32)
                solved[second, columns] = jnp.where(front == 2 * group + 1, kept, result[OWN:]).astype(BF16)

                @pl.when(front < last)
                def _():
                    copy_fwd(group, index).start()

        @pl.when(jnp.logical_and(front == 2 * group, front > 0))
        def _():
            for index in range(CHUNKS):
                copy_fwd(group, index).start()

    def send_entries(half):
        columns = pl.ds(half * HALF, HALF)
        entries[half, own_part(front)] = dot_last(own[...], back[columns, :])
        for step in (4, 5, 3, 2, 6, 7, 1):
            copy_entry(half, step, front).start()

    def backward(group):
        rows = rows_of(group)
        for index in range(CHUNKS):
            columns = chunk_lanes(index)

            @pl.when(front < last)
            def _():
                copy_bwd(group, index).wait_recv()

            upper = solved[rows, columns].astype(F32)
            lower = handed_in[rows, columns].astype(F32)
            back[rows, columns] = jnp.where(front == last, upper, upper - lower).astype(BF16)

            @pl.when(front > 0)
            def _():
                total = dot_wide(back[rows, columns], inverse[columns, :])
                if index > 0:
                    total = displaced[rows, :] + total
                displaced[rows, :] = total
                if index == CHUNKS - 1:
                    reduced[...] = total.astype(BF16)

            @pl.when(front == 0)
            def _():
                part = dot_wide(back[rows, columns], modal_map[columns, :])
                modal_out[rows, :] = part if index == 0 else modal_out[rows, :] + part

        @pl.when(front > 0)
        def _():
            for index in range(CHUNKS):
                columns = chunk_lanes(index)
                handed[rows, columns] = dot_wide(reduced[...], coupling[:, columns]).astype(BF16)
                copy_bwd(group, index).start()

            modal_out[rows, :] = dot_wide(reduced[...], modal_map[...])

        @pl.when(front < last)
        def _():
            copy_sum(group).wait_recv()
            modal_out[rows, :] = modal_out[rows, :] + modal_in[rows, :]

        @pl.when(front > 0)
        def _():
            copy_sum(group).start()

        @pl.when(front == 0)
        def _():
            modal[rows, :] = modal_out[rows, :].astype(BF16)
            for step in (4, 5, 3, 2, 6, 7, 1):
                copy_modal(group, step).start()

        @pl.when(group == 2)
        def _():
            send_entries(1)

    build_modal_at = jnp.where(
        front < 5, jnp.maximum(2 * front + 1, 5), jnp.where(front < last, 1, 0)
    )
    build_picks_at = jnp.where(front < 4, 9, 99)
    shift = jnp.where(front == last, 1, -1)

    def slot(moment, carry):
        @pl.when(moment == build_modal_at)
        def _():
            build_modal_map()

        @pl.when(moment == build_picks_at)
        def _():
            build_picks()

        even = lax.rem(moment, 2) == 0
        ahead = front - moment // 2
        behind = 15 - front - (moment + shift) // 2

        @pl.when(jnp.logical_and(even, jnp.logical_and(ahead >= 0, lax.rem(ahead + 32, 2) == 0)))
        def _():
            forward(ahead // 2)

        @pl.when(
            jnp.logical_and(
                jnp.logical_not(even),
                jnp.logical_and(
                    jnp.logical_and(behind >= 0, behind < 2 * GROUPS), lax.rem(behind + 32, 2) == 0
                ),
            )
        )
        def _():
            backward(behind // 2)

        return carry

    lax.fori_loop(0, 32, slot, 0)
    send_entries(0)

    @pl.when(front >= 4)
    def _():
        build_picks()

    real = slice(0, COLS)

    @pl.when(front > 0)
    def _():
        for group in range(GROUPS):
            copy_modal(group, 1).wait_recv()

    def wait_rows(step, carry):
        copy_mode(step, peer_front(step)).wait_recv()
        copy_entry(0, step, peer_front(step)).wait_recv()
        copy_entry(1, step, peer_front(step)).wait_recv()
        return carry

    lax.fori_loop(1, FRONTS, wait_rows, 0)
    projected = dot_last(mode_rows[...], modal[real, :])
    for half in range(2):
        lanes = slice(half * HALF, (half + 1) * HALF)
        flexible = (entries[half] - projected[:, lanes]).astype(BF16)
        rows_out[:, :, lanes] = dot(route[...], flexible).astype(BF16).reshape(SUBS, SHARE, HALF)

    def send_row(step, carry):
        copy_row(step, sub).start()
        return carry

    lax.fori_loop(1, subs, send_row, 0)
    rows_in[sub] = rows_out[sub]

    @pl.when(front == 0)
    def _():
        def displace(index, carry):
            columns = chunk(index)
            displaced[:, columns] = dot(back[...], inverse[:, columns])
            return carry

        lax.fori_loop(0, CHUNKS, displace, 0)

    def deflate(index, carry):
        columns = chunk(index)
        attachment[:, columns] = (
            displaced[real, columns] - dot(modal[real, :], modes[:, columns])
        ).astype(BF16)
        return carry

    lax.fori_loop(0, CHUNKS, deflate, 0)
    store = pltpu.make_async_copy(attachment, attachment_hbm.at[0], store_sem.at[0])
    store.start()

    high_place = lax.broadcasted_iota(jnp.int32, (SUBS, SHARE, COLS), 0)
    total = jnp.zeros((SUBS * SHARE, 128), F32)
    for step in range(subs):
        source = peer_sub(step)
        if step > 0:
            copy_row(step, source).wait_recv()
        level = lax.shift_right_logical(ids_ref[pl.ds(source, 1), :], 7)
        chosen = jnp.where(
            high_place == level[:, None, :], rows_in[source].astype(F32)[None, :, :], 0.0
        ).astype(BF16)
        total = total + dot_last(chosen.reshape(SUBS * SHARE, COLS), low_pick[source])
    for index in range(SUBS):
        flexibility[:, index * 128 : (index + 1) * 128] = total[index * SHARE : (index + 1) * SHARE]
    store_flexibility = pltpu.make_async_copy(flexibility, flexibility_hbm, store_sem.at[1])
    store_flexibility.start()

    for group in range(GROUPS):

        @pl.when(jnp.logical_and(front < last, front >= 2 * group))
        def _():
            copy_fwd(group, 0, whole).wait_send()

        @pl.when(front > 0)
        def _():
            copy_bwd(group, 0, whole).wait_send()
            copy_sum(group).wait_send()

        @pl.when(front == 0)
        def _():
            for step in range(1, FRONTS):
                copy_modal(group, step).wait_send()

    def wait_sends(step, carry):
        copy_mode(step, front).wait_send()
        copy_entry(0, step, front).wait_send()
        copy_entry(1, step, front).wait_send()
        return carry

    lax.fori_loop(1, FRONTS, wait_sends, 0)

    def wait_row_sends(step, carry):
        copy_row(step, sub).wait_send()
        return carry

    lax.fori_loop(1, subs, wait_row_sends, 0)
    store.wait()
    store_flexibility.wait()


def on_device(front_inverse, coupling, free_modes, dof_offset, interface_id):
    dma = pltpu.SemaphoreType.DMA
    vmem = pltpu.VMEM
    anywhere = pl.BlockSpec(memory_space=pl.ANY)
    local = pl.BlockSpec(memory_space=pltpu.VMEM)
    return pl.pallas_call(
        kernel,
        out_shape=(
            jax.ShapeDtypeStruct((1, COLS, NF), BF16),
            jax.ShapeDtypeStruct((SHARE, NF), F32),
        ),
        in_specs=[anywhere, anywhere, anywhere, local, local],
        out_specs=(anywhere, anywhere),
        scratch_shapes=[
            vmem((NF, NF), BF16),
            vmem((NF, NF), BF16),
            vmem((MODES, NF), BF16),
            vmem((MPAD, NF), BF16),
            vmem((NF, NF), BF16),
            vmem((NF, NF), BF16),
            vmem((NF, MPAD), BF16),
            vmem((WIDTH, NF), F32),
            vmem((OWN, NF), BF16),
            vmem((OWN, NF), BF16),
            vmem((COLS, NF), BF16),
            vmem((COLS, NF), BF16),
            vmem((WIDTH, NF), BF16),
            vmem((COLS, NF), BF16),
            vmem((COLS, NF), BF16),
            vmem((COLS, NF), BF16),
            vmem((COLS, MPAD), F32),
            vmem((COLS, MPAD), F32),
            vmem((COLS, MPAD), BF16),
            vmem((COLS, MPAD), BF16),
            vmem((2, COLS, HALF), F32),
            vmem((COLS, COLS), BF16),
            vmem((SUBS, SHARE, COLS), BF16),
            vmem((SUBS, SHARE, COLS), BF16),
            vmem((SUBS, 128, COLS), BF16),
            vmem((COLS, NF), F32),
            vmem((COLS, NF), BF16),
            vmem((SHARE, NF), F32),
            dma((CHUNKS,)),
            dma((CHUNKS,)),
            dma,
            dma((GROUPS,)),
            dma((GROUPS, CHUNKS)),
            dma((GROUPS,)),
            dma((GROUPS, CHUNKS)),
            dma((GROUPS,)),
            dma((GROUPS,)),
            dma((GROUPS, FRONTS)),
            dma((GROUPS,)),
            dma((FRONTS,)),
            dma((FRONTS,)),
            dma((2, FRONTS)),
            dma((2, FRONTS)),
            dma((SUBS,)),
            dma((SUBS,)),
            dma((2,)),
        ],
        compiler_params=pltpu.CompilerParams(
            collective_id=0, has_side_effects=True, vmem_limit_bytes=60 << 20
        ),
        name="chain",
    )(front_inverse, coupling, free_modes, dof_offset, interface_id)


def solution(mesh):
    return jax.shard_map(
        on_device,
        mesh=mesh,
        in_specs=(
            P("sub", "front", None),
            P("sub", "front", None),
            P("sub", None, "front"),
            P("sub", "front"),
            P(),
        ),
        out_specs=(P("sub", None, "front"), P(("sub", "front"), None)),
        check_vma=False,
    )
```

```python
import functools

import jax
import jax.numpy as jnp
from jax import lax
from jax.experimental import pallas as pl
from jax.experimental.pallas import tpu as pltpu
from jax.sharding import PartitionSpec as P

MESH = pl.DeviceIdType.MESH
F32 = jnp.float32
BF16 = jnp.bfloat16

FRONTS = 8
SUBS = 16
NF = 2048
COLS = 256
OWN = 32
GROUPS = 4
WIDTH = 64
CHUNK = 512
CHUNKS = NF // CHUNK
MODES = 300
MPAD = 384
SHARE = 16
HALF = COLS // 2


def dot(left, right):
    return jnp.dot(left, right, preferred_element_type=F32)


def dot_last(left, right):
    return lax.dot_general(left, right, (((1,), (1,)), ((), ())), preferred_element_type=F32)


def dot_wide(left, right):
    count = left.shape[0]
    if count < 128:
        left = jnp.concatenate([left, left, left, left][: 128 // count] + [left[: 128 % count]] * (128 % count > 0), axis=0)
    return dot(left, right)[:count]


def tile(index, size):
    return pl.ds(pl.multiple_of(index * size, size), size)


def kernel(
    inverse_hbm,
    coupling_hbm,
    modes_hbm,
    offsets_ref,
    ids_ref,
    attachment_hbm,
    flexibility_hbm,
    inverse,
    coupling,
    modes_raw,
    modes,
    turned,
    coupling_turned,
    modal_map,
    gathered,
    pick,
    own,
    solved,
    solved_in,
    reduced,
    back,
    handed,
    handed_in,
    modal_out,
    modal_in,
    modal,
    mode_rows,
    entries,
    route,
    rows_out,
    rows_in,
    low_pick,
    placed,
    displaced,
    attachment,
    flexibility,
    inverse_sem,
    coupling_sem,
    modes_sem,
    fwd_send,
    fwd_recv,
    bwd_send,
    bwd_recv,
    sum_send,
    sum_recv,
    modal_send,
    modal_recv,
    mode_send,
    mode_recv,
    entry_send,
    entry_recv,
    row_send,
    row_recv,
    store_sem,
):
    front = lax.axis_index("front")
    sub = lax.axis_index("sub")
    subs = lax.axis_size("sub")
    last = FRONTS - 1

    def chunk(index):
        return tile(index, CHUNK)

    def load_inverse(index):
        rows = chunk(index)
        return pltpu.make_async_copy(inverse_hbm.at[0, rows], inverse.at[rows], inverse_sem.at[index])

    def load_coupling(index):
        rows = chunk(index)
        return pltpu.make_async_copy(coupling_hbm.at[0, rows], coupling.at[rows], coupling_sem.at[index])

    load_modes = pltpu.make_async_copy(modes_hbm.at[0], modes_raw, modes_sem)
    for index in range(CHUNKS):
        load_inverse(index).start()

    def peer_front(step):
        return lax.rem(front + step, FRONTS)

    def peer_sub(step):
        return lax.rem(sub + step, subs)

    barrier = pltpu.get_barrier_semaphore()

    def greet_front(step, carry):
        pl.semaphore_signal(barrier, inc=1, device_id={"front": peer_front(step)}, device_id_type=MESH)
        return carry

    def greet_sub(step, carry):
        pl.semaphore_signal(barrier, inc=1, device_id={"sub": peer_sub(step)}, device_id_type=MESH)
        return carry

    lax.fori_loop(1, FRONTS, greet_front, 0)
    lax.fori_loop(1, subs, greet_sub, 0)

    offsets_square = jnp.broadcast_to(offsets_ref[...].astype(F32), (OWN, OWN))
    diagonal = lax.broadcasted_iota(jnp.int32, (OWN, OWN), 0) == lax.broadcasted_iota(
        jnp.int32, (OWN, OWN), 1
    )
    offsets_column = jnp.sum(
        jnp.where(diagonal, offsets_square, 0.0), axis=1, keepdims=True
    ).astype(jnp.int32)
    pick[...] = (offsets_column == lax.broadcasted_iota(jnp.int32, (OWN, NF), 1)).astype(F32).astype(BF16)
    solved[...] = jnp.zeros((COLS, NF), BF16)

    @pl.when(front == 0)
    def _():
        def one(index, carry):
            load_inverse(index).wait()
            load_coupling(index).start()
            own[:, chunk(index)] = dot_last(pick[...], inverse[chunk(index), :]).astype(BF16)
            return carry

        lax.fori_loop(0, CHUNKS, one, 0)

    @pl.when(front > 0)
    def _():
        def one(index, carry):
            load_inverse(index).wait()
            load_coupling(index).start()
            block = inverse[chunk(index), :].T
            turned[:, chunk(index)] = block
            own[:, chunk(index)] = dot(pick[...], block).astype(BF16)
            return carry

        lax.fori_loop(0, CHUNKS, one, 0)

    load_modes.start()
    own_rows = pl.ds(pl.multiple_of(front * OWN, OWN), OWN)
    solved[own_rows, :] = own[...]
    pl.semaphore_wait(barrier, FRONTS - 1 + subs - 1)

    def rows_of(group):
        return tile(group, WIDTH)

    after = jnp.minimum(front + 1, last)
    before = jnp.maximum(front - 1, 0)
    whole = slice(0, NF)

    def chunk_lanes(index):
        return slice(index * CHUNK, (index + 1) * CHUNK)

    def copy_fwd(group, index, columns=None):
        columns = chunk_lanes(index) if columns is None else columns
        return pltpu.make_async_remote_copy(
            src_ref=solved.at[rows_of(group), columns],
            dst_ref=solved_in.at[rows_of(group), columns],
            send_sem=fwd_send.at[group],
            recv_sem=fwd_recv.at[group, index],
            device_id={"front": after},
            device_id_type=MESH,
        )

    def copy_bwd(group, index, columns=None):
        columns = chunk_lanes(index) if columns is None else columns
        return pltpu.make_async_remote_copy(
            src_ref=handed.at[rows_of(group), columns],
            dst_ref=handed_in.at[rows_of(group), columns],
            send_sem=bwd_send.at[group],
            recv_sem=bwd_recv.at[group, index],
            device_id={"front": before},
            device_id_type=MESH,
        )

    def copy_sum(group):
        return pltpu.make_async_remote_copy(
            src_ref=modal_out.at[rows_of(group)],
            dst_ref=modal_in.at[rows_of(group)],
            send_sem=sum_send.at[group],
            recv_sem=sum_recv.at[group],
            device_id={"front": before},
            device_id_type=MESH,
        )

    def copy_modal(group, step):
        return pltpu.make_async_remote_copy(
            src_ref=modal.at[rows_of(group)],
            dst_ref=modal.at[rows_of(group)],
            send_sem=modal_send.at[group, step],
            recv_sem=modal_recv.at[group],
            device_id={"front": peer_front(step)},
            device_id_type=MESH,
        )

    def own_part(index):
        return pl.ds(pl.multiple_of(index * OWN, OWN), OWN)

    def copy_mode(step, index):
        rows = own_part(index)
        return pltpu.make_async_remote_copy(
            src_ref=mode_rows.at[rows],
            dst_ref=mode_rows.at[rows],
            send_sem=mode_send.at[step],
            recv_sem=mode_recv.at[index],
            device_id={"front": peer_front(step)},
            device_id_type=MESH,
        )

    def copy_entry(half, step, index):
        rows = own_part(index)
        return pltpu.make_async_remote_copy(
            src_ref=entries.at[half, rows],
            dst_ref=entries.at[half, rows],
            send_sem=entry_send.at[half, step],
            recv_sem=entry_recv.at[half, index],
            device_id={"front": peer_front(step)},
            device_id_type=MESH,
        )

    def copy_row(step, source):
        return pltpu.make_async_remote_copy(
            src_ref=rows_out.at[peer_sub(step)],
            dst_ref=rows_in.at[source],
            send_sem=row_send.at[step],
            recv_sem=row_recv.at[source],
            device_id={"sub": peer_sub(step)},
            device_id_type=MESH,
        )

    @pl.when(front == 0)
    def _():
        for index in range(CHUNKS):
            copy_fwd(0, index).start()

    @pl.when(front > 0)
    def _():
        def one(index, carry):
            load_coupling(index).wait()
            coupling_turned[:, chunk(index)] = coupling[chunk(index), :].T
            return carry

        lax.fori_loop(0, CHUNKS, one, 0)

    @pl.when(front == 0)
    def _():
        def one(index, carry):
            load_coupling(index).wait()
            return carry

        lax.fori_loop(0, CHUNKS, one, 0)

    def build_modal_map():
        load_modes.wait()
        modes[...] = jnp.zeros((MPAD, NF), BF16)
        modes[pl.ds(0, MODES), :] = modes_raw[...]

        @pl.when(front == 0)
        def _():
            def one(index, carry):
                rows = chunk(index)
                modal_map[rows, :] = dot_last(inverse[rows, :], modes[...]).astype(BF16)
                return carry

            lax.fori_loop(0, CHUNKS, one, 0)

        @pl.when(front > 0)
        def _():
            def one(index, carry):
                rows = chunk(index)
                modal_map[rows, :] = modes[:, rows].T
                return carry

            lax.fori_loop(0, CHUNKS, one, 0)

    def build_picks():
        mode_rows[own_part(front), :] = dot_last(pick[...], modes[...]).astype(BF16)

        def send(step, carry):
            copy_mode(step, front).start()
            return carry

        lax.fori_loop(1, FRONTS, send, 0)

        place = lax.broadcasted_iota(jnp.int32, (COLS, COLS), 0)
        target = (
            lax.shift_right_logical(place, 4) * (FRONTS * SHARE)
            + jnp.bitwise_and(place, 15)
            + front * SHARE
        )
        route[...] = (target == ids_ref[pl.ds(sub, 1), :]).astype(F32).astype(BF16)
        lane_place = lax.broadcasted_iota(jnp.int32, (128, COLS), 0)

        def fill_low(index, carry):
            ids = jnp.bitwise_and(ids_ref[pl.ds(index, 1), :], 127)
            low_pick[:, tile(index, COLS)] = (lane_place == ids).astype(F32).astype(BF16)
            return carry

        lax.fori_loop(0, SUBS, fill_low, 0)

    def forward(group):
        rows = rows_of(group)

        @pl.when(front > 2 * group)
        def _():
            for index in range(CHUNKS):
                columns = chunk_lanes(index)
                copy_fwd(group, index).wait_recv()
                part = dot_wide(solved_in[rows, columns], coupling_turned[columns, :])
                if index == 0:
                    gathered[...] = part
                elif index < CHUNKS - 1:
                    gathered[...] = gathered[...] + part
                else:
                    reduced[...] = (gathered[...] + part).astype(BF16)

            first = tile(2 * group, OWN)
            second = tile(2 * group + 1, OWN)
            for index in range(CHUNKS):
                columns = chunk_lanes(index)
                result = 0.0 - dot_wide(reduced[...], turned[:, columns])
                solved[first, columns] = result[:OWN].astype(BF16)
                kept = solved[second, columns].astype(F32)
                solved[second, columns] = jnp.where(front == 2 * group + 1, kept, result[OWN:]).astype(BF16)

                @pl.when(front < last)
                def _():
                    copy_fwd(group, index).start()

        @pl.when(jnp.logical_and(front == 2 * group, front > 0))
        def _():
            for index in range(CHUNKS):
                copy_fwd(group, index).start()

    def send_entries(half):
        columns = pl.ds(half * HALF, HALF)
        entries[half, own_part(front)] = dot_last(own[...], back[columns, :])
        for step in (4, 5, 3, 2, 6, 7, 1):
            copy_entry(half, step, front).start()

    def displace_rows(group):
        rows = rows_of(group)

        def one(index, carry):
            columns = tile(index, 2 * CHUNK)
            displaced[rows, columns] = dot_wide(back[rows, :], inverse[:, columns])
            return carry

        lax.fori_loop(0, CHUNKS // 2, one, 0)

    def backward(group):
        rows = rows_of(group)
        for index in range(CHUNKS):
            columns = chunk_lanes(index)

            @pl.when(front < last)
            def _():
                copy_bwd(group, index).wait_recv()

            upper = solved[rows, columns].astype(F32)
            lower = handed_in[rows, columns].astype(F32)
            back[rows, columns] = jnp.where(front == last, upper, upper - lower).astype(BF16)

            @pl.when(front > 0)
            def _():
                total = dot_wide(back[rows, columns], inverse[columns, :])
                if index > 0:
                    total = displaced[rows, :] + total
                displaced[rows, :] = total
                if index == CHUNKS - 1:
                    reduced[...] = total.astype(BF16)

            @pl.when(front == 0)
            def _():
                part = dot_wide(back[rows, columns], modal_map[columns, :])
                modal_out[rows, :] = part if index == 0 else modal_out[rows, :] + part

        @pl.when(front > 0)
        def _():
            for index in range(CHUNKS):
                columns = chunk_lanes(index)
                handed[rows, columns] = dot_wide(reduced[...], coupling[:, columns]).astype(BF16)
                copy_bwd(group, index).start()

            modal_out[rows, :] = dot_wide(reduced[...], modal_map[...])

        @pl.when(front < last)
        def _():
            copy_sum(group).wait_recv()
            modal_out[rows, :] = modal_out[rows, :] + modal_in[rows, :]

        @pl.when(front > 0)
        def _():
            copy_sum(group).start()

        @pl.when(front == 0)
        def _():
            modal[rows, :] = modal_out[rows, :].astype(BF16)
            for step in (4, 5, 3, 2, 6, 7, 1):
                copy_modal(group, step).start()

        @pl.when(jnp.logical_and(front == 0, group > 0))
        def _():
            displace_rows(group)

        @pl.when(group == 2)
        def _():
            send_entries(1)

    build_modal_at = jnp.where(
        front < 5, jnp.maximum(2 * front + 1, 5), jnp.where(front < last, 1, 0)
    )
    build_picks_at = jnp.where(front < 4, 9, 99)
    shift = jnp.where(front == last, 1, -1)

    def slot(moment, carry):
        @pl.when(moment == build_modal_at)
        def _():
            build_modal_map()

        @pl.when(moment == build_picks_at)
        def _():
            build_picks()

        even = lax.rem(moment, 2) == 0
        ahead = front - moment // 2
        behind = 15 - front - (moment + shift) // 2

        @pl.when(jnp.logical_and(even, jnp.logical_and(ahead >= 0, lax.rem(ahead + 32, 2) == 0)))
        def _():
            forward(ahead // 2)

        @pl.when(
            jnp.logical_and(
                jnp.logical_not(even),
                jnp.logical_and(
                    jnp.logical_and(behind >= 0, behind < 2 * GROUPS), lax.rem(behind + 32, 2) == 0
                ),
            )
        )
        def _():
            backward(behind // 2)

        return carry

    lax.fori_loop(0, 32, slot, 0)
    send_entries(0)

    @pl.when(front == 0)
    def _():
        displace_rows(0)

    @pl.when(front >= 4)
    def _():
        build_picks()

    real = slice(0, COLS)

    @pl.when(front > 0)
    def _():
        for group in range(GROUPS):
            copy_modal(group, 1).wait_recv()

    def wait_rows(step, carry):
        copy_mode(step, peer_front(step)).wait_recv()
        copy_entry(0, step, peer_front(step)).wait_recv()
        copy_entry(1, step, peer_front(step)).wait_recv()
        return carry

    lax.fori_loop(1, FRONTS, wait_rows, 0)
    projected = dot_last(mode_rows[...], modal[real, :])
    for half in range(2):
        lanes = slice(half * HALF, (half + 1) * HALF)
        flexible = (entries[half] - projected[:, lanes]).astype(BF16)
        rows_out[:, :, lanes] = dot(route[...], flexible).astype(BF16).reshape(SUBS, SHARE, HALF)

    def send_row(step, carry):
        copy_row(step, sub).start()
        return carry

    lax.fori_loop(1, subs, send_row, 0)
    rows_in[sub] = rows_out[sub]

    def deflate(index, carry):
        columns = chunk(index)
        attachment[:, columns] = (
            displaced[real, columns] - dot(modal[real, :], modes[:, columns])
        ).astype(BF16)
        return carry

    lax.fori_loop(0, CHUNKS, deflate, 0)
    store = pltpu.make_async_copy(attachment, attachment_hbm.at[0], store_sem.at[0])
    store.start()

    def wait_row(step, carry):
        copy_row(step, peer_sub(step)).wait_recv()
        return carry

    lax.fori_loop(1, subs, wait_row, 0)
    high_place = lax.broadcasted_iota(jnp.int32, (SUBS, SHARE, COLS), 0)
    for index in range(SUBS):
        level = lax.shift_right_logical(ids_ref[index : index + 1, :], 7)
        chosen = jnp.where(
            high_place == level[:, None, :], rows_in[index].astype(F32)[None, :, :], 0.0
        ).astype(BF16)
        placed[:, index * COLS : (index + 1) * COLS] = chosen.reshape(SUBS * SHARE, COLS)
    total = dot_last(placed[...], low_pick[...])
    for index in range(SUBS):
        flexibility[:, index * 128 : (index + 1) * 128] = total[index * SHARE : (index + 1) * SHARE]
    store_flexibility = pltpu.make_async_copy(flexibility, flexibility_hbm, store_sem.at[1])
    store_flexibility.start()

    for group in range(GROUPS):

        @pl.when(jnp.logical_and(front < last, front >= 2 * group))
        def _():
            copy_fwd(group, 0, whole).wait_send()

        @pl.when(front > 0)
        def _():
            copy_bwd(group, 0, whole).wait_send()
            copy_sum(group).wait_send()

        @pl.when(front == 0)
        def _():
            for step in range(1, FRONTS):
                copy_modal(group, step).wait_send()

    def wait_sends(step, carry):
        copy_mode(step, front).wait_send()
        copy_entry(0, step, front).wait_send()
        copy_entry(1, step, front).wait_send()
        return carry

    lax.fori_loop(1, FRONTS, wait_sends, 0)

    def wait_row_sends(step, carry):
        copy_row(step, sub).wait_send()
        return carry

    lax.fori_loop(1, subs, wait_row_sends, 0)
    store.wait()
    store_flexibility.wait()


def on_device(front_inverse, coupling, free_modes, dof_offset, interface_id):
    dma = pltpu.SemaphoreType.DMA
    vmem = pltpu.VMEM
    anywhere = pl.BlockSpec(memory_space=pl.ANY)
    local = pl.BlockSpec(memory_space=pltpu.VMEM)
    return pl.pallas_call(
        kernel,
        out_shape=(
            jax.ShapeDtypeStruct((1, COLS, NF), BF16),
            jax.ShapeDtypeStruct((SHARE, NF), F32),
        ),
        in_specs=[anywhere, anywhere, anywhere, local, local],
        out_specs=(anywhere, anywhere),
        scratch_shapes=[
            vmem((NF, NF), BF16),
            vmem((NF, NF), BF16),
            vmem((MODES, NF), BF16),
            vmem((MPAD, NF), BF16),
            vmem((NF, NF), BF16),
            vmem((NF, NF), BF16),
            vmem((NF, MPAD), BF16),
            vmem((WIDTH, NF), F32),
            vmem((OWN, NF), BF16),
            vmem((OWN, NF), BF16),
            vmem((COLS, NF), BF16),
            vmem((COLS, NF), BF16),
            vmem((WIDTH, NF), BF16),
            vmem((COLS, NF), BF16),
            vmem((COLS, NF), BF16),
            vmem((COLS, NF), BF16),
            vmem((COLS, MPAD), F32),
            vmem((COLS, MPAD), F32),
            vmem((COLS, MPAD), BF16),
            vmem((COLS, MPAD), BF16),
            vmem((2, COLS, HALF), F32),
            vmem((COLS, COLS), BF16),
            vmem((SUBS, SHARE, COLS), BF16),
            vmem((SUBS, SHARE, COLS), BF16),
            vmem((128, SUBS * COLS), BF16),
            vmem((SUBS * SHARE, SUBS * COLS), BF16),
            vmem((COLS, NF), F32),
            vmem((COLS, NF), BF16),
            vmem((SHARE, NF), F32),
            dma((CHUNKS,)),
            dma((CHUNKS,)),
            dma,
            dma((GROUPS,)),
            dma((GROUPS, CHUNKS)),
            dma((GROUPS,)),
            dma((GROUPS, CHUNKS)),
            dma((GROUPS,)),
            dma((GROUPS,)),
            dma((GROUPS, FRONTS)),
            dma((GROUPS,)),
            dma((FRONTS,)),
            dma((FRONTS,)),
            dma((2, FRONTS)),
            dma((2, FRONTS)),
            dma((SUBS,)),
            dma((SUBS,)),
            dma((2,)),
        ],
        compiler_params=pltpu.CompilerParams(
            collective_id=0, has_side_effects=True, vmem_limit_bytes=60 << 20
        ),
        name="chain",
    )(front_inverse, coupling, free_modes, dof_offset, interface_id)


def solution(mesh):
    return jax.shard_map(
        on_device,
        mesh=mesh,
        in_specs=(
            P("sub", "front", None),
            P("sub", "front", None),
            P("sub", None, "front"),
            P("sub", "front"),
            P(),
        ),
        out_specs=(P("sub", None, "front"), P(("sub", "front"), None)),
        check_vma=False,
    )
```

```python
import functools

import jax
import jax.numpy as jnp
from jax import lax
from jax.experimental import pallas as pl
from jax.experimental.pallas import tpu as pltpu
from jax.sharding import PartitionSpec as P

MESH = pl.DeviceIdType.MESH
F32 = jnp.float32
BF16 = jnp.bfloat16

FRONTS = 8
SUBS = 16
NF = 2048
COLS = 256
OWN = 32
GROUPS = 4
WIDTH = 64
CHUNK = 512
CHUNKS = NF // CHUNK
MODES = 300
MPAD = 384
SHARE = 16
HALF = COLS // 2


def dot(left, right):
    return jnp.dot(left, right, preferred_element_type=F32)


def dot_last(left, right):
    return lax.dot_general(left, right, (((1,), (1,)), ((), ())), preferred_element_type=F32)


def dot_wide(left, right):
    count = left.shape[0]
    if count < 128:
        left = jnp.concatenate([left, left, left, left][: 128 // count] + [left[: 128 % count]] * (128 % count > 0), axis=0)
    return dot(left, right)[:count]


def tile(index, size):
    return pl.ds(pl.multiple_of(index * size, size), size)


def kernel(
    inverse_hbm,
    coupling_hbm,
    modes_hbm,
    offsets_ref,
    ids_ref,
    attachment_hbm,
    flexibility_hbm,
    inverse,
    coupling,
    modes_raw,
    modes,
    turned,
    coupling_turned,
    modal_map,
    gathered,
    pick,
    own,
    solved,
    solved_in,
    reduced,
    back,
    handed,
    handed_in,
    modal_out,
    modal_part,
    modal_in,
    modal,
    mode_rows,
    entries,
    route,
    rows_out,
    rows_in,
    low_pick,
    placed,
    displaced,
    attachment,
    flexibility,
    inverse_sem,
    coupling_sem,
    modes_sem,
    fwd_send,
    fwd_recv,
    bwd_send,
    bwd_recv,
    sum_send,
    sum_recv,
    modal_send,
    modal_recv,
    mode_send,
    mode_recv,
    entry_send,
    entry_recv,
    row_send,
    row_recv,
    store_sem,
):
    front = lax.axis_index("front")
    sub = lax.axis_index("sub")
    subs = lax.axis_size("sub")
    last = FRONTS - 1

    def chunk(index):
        return tile(index, CHUNK)

    def load_inverse(index):
        rows = chunk(index)
        return pltpu.make_async_copy(inverse_hbm.at[0, rows], inverse.at[rows], inverse_sem.at[index])

    def load_coupling(index):
        rows = chunk(index)
        return pltpu.make_async_copy(coupling_hbm.at[0, rows], coupling.at[rows], coupling_sem.at[index])

    load_modes = pltpu.make_async_copy(modes_hbm.at[0], modes_raw, modes_sem)
    for index in range(CHUNKS):
        load_inverse(index).start()

    def peer_front(step):
        return lax.rem(front + step, FRONTS)

    def peer_sub(step):
        return lax.rem(sub + step, subs)

    barrier = pltpu.get_barrier_semaphore()

    def greet_front(step, carry):
        pl.semaphore_signal(barrier, inc=1, device_id={"front": peer_front(step)}, device_id_type=MESH)
        return carry

    def greet_sub(step, carry):
        pl.semaphore_signal(barrier, inc=1, device_id={"sub": peer_sub(step)}, device_id_type=MESH)
        return carry

    lax.fori_loop(1, FRONTS, greet_front, 0)
    lax.fori_loop(1, subs, greet_sub, 0)

    offsets_square = jnp.broadcast_to(offsets_ref[...].astype(F32), (OWN, OWN))
    diagonal = lax.broadcasted_iota(jnp.int32, (OWN, OWN), 0) == lax.broadcasted_iota(
        jnp.int32, (OWN, OWN), 1
    )
    offsets_column = jnp.sum(
        jnp.where(diagonal, offsets_square, 0.0), axis=1, keepdims=True
    ).astype(jnp.int32)
    pick[...] = (offsets_column == lax.broadcasted_iota(jnp.int32, (OWN, NF), 1)).astype(F32).astype(BF16)
    solved[...] = jnp.zeros((COLS, NF), BF16)

    @pl.when(front == 0)
    def _():
        def one(index, carry):
            load_inverse(index).wait()
            load_coupling(index).start()
            own[:, chunk(index)] = dot_last(pick[...], inverse[chunk(index), :]).astype(BF16)
            return carry

        lax.fori_loop(0, CHUNKS, one, 0)

    @pl.when(front > 0)
    def _():
        def one(index, carry):
            load_inverse(index).wait()
            load_coupling(index).start()
            block = inverse[chunk(index), :].T
            turned[:, chunk(index)] = block
            own[:, chunk(index)] = dot(pick[...], block).astype(BF16)
            return carry

        lax.fori_loop(0, CHUNKS, one, 0)

    load_modes.start()
    own_rows = pl.ds(pl.multiple_of(front * OWN, OWN), OWN)
    solved[own_rows, :] = own[...]
    pl.semaphore_wait(barrier, FRONTS - 1 + subs - 1)

    def rows_of(group):
        return tile(group, WIDTH)

    after = jnp.minimum(front + 1, last)
    before = jnp.maximum(front - 1, 0)
    whole = slice(0, NF)

    def chunk_lanes(index):
        return slice(index * CHUNK, (index + 1) * CHUNK)

    def copy_fwd(group, index, columns=None):
        columns = chunk_lanes(index) if columns is None else columns
        return pltpu.make_async_remote_copy(
            src_ref=solved.at[rows_of(group), columns],
            dst_ref=solved_in.at[rows_of(group), columns],
            send_sem=fwd_send.at[group],
            recv_sem=fwd_recv.at[group, index],
            device_id={"front": after},
            device_id_type=MESH,
        )

    def copy_bwd(group, index, columns=None):
        columns = chunk_lanes(index) if columns is None else columns
        return pltpu.make_async_remote_copy(
            src_ref=handed.at[rows_of(group), columns],
            dst_ref=handed_in.at[rows_of(group), columns],
            send_sem=bwd_send.at[group],
            recv_sem=bwd_recv.at[group, index],
            device_id={"front": before},
            device_id_type=MESH,
        )

    def copy_sum(group):
        return pltpu.make_async_remote_copy(
            src_ref=modal_part.at[rows_of(group)],
            dst_ref=modal_in.at[rows_of(group)],
            send_sem=sum_send.at[group],
            recv_sem=sum_recv.at[group],
            device_id={"front": before},
            device_id_type=MESH,
        )

    def copy_modal(group, step):
        return pltpu.make_async_remote_copy(
            src_ref=modal.at[rows_of(group)],
            dst_ref=modal.at[rows_of(group)],
            send_sem=modal_send.at[group, step],
            recv_sem=modal_recv.at[group],
            device_id={"front": peer_front(step)},
            device_id_type=MESH,
        )

    def own_part(index):
        return pl.ds(pl.multiple_of(index * OWN, OWN), OWN)

    def copy_mode(step, index):
        rows = own_part(index)
        return pltpu.make_async_remote_copy(
            src_ref=mode_rows.at[rows],
            dst_ref=mode_rows.at[rows],
            send_sem=mode_send.at[step],
            recv_sem=mode_recv.at[index],
            device_id={"front": peer_front(step)},
            device_id_type=MESH,
        )

    def copy_entry(half, step, index):
        rows = own_part(index)
        return pltpu.make_async_remote_copy(
            src_ref=entries.at[half, rows],
            dst_ref=entries.at[half, rows],
            send_sem=entry_send.at[half, step],
            recv_sem=entry_recv.at[half, index],
            device_id={"front": peer_front(step)},
            device_id_type=MESH,
        )

    def copy_row(step, source):
        return pltpu.make_async_remote_copy(
            src_ref=rows_out.at[peer_sub(step)],
            dst_ref=rows_in.at[source],
            send_sem=row_send.at[step],
            recv_sem=row_recv.at[source],
            device_id={"sub": peer_sub(step)},
            device_id_type=MESH,
        )

    @pl.when(front == 0)
    def _():
        for index in range(CHUNKS):
            copy_fwd(0, index).start()

    @pl.when(front > 0)
    def _():
        def one(index, carry):
            load_coupling(index).wait()
            coupling_turned[:, chunk(index)] = coupling[chunk(index), :].T
            return carry

        lax.fori_loop(0, CHUNKS, one, 0)

    @pl.when(front == 0)
    def _():
        def one(index, carry):
            load_coupling(index).wait()
            return carry

        lax.fori_loop(0, CHUNKS, one, 0)

    def build_modal_map():
        load_modes.wait()
        modes[...] = jnp.zeros((MPAD, NF), BF16)
        modes[pl.ds(0, MODES), :] = modes_raw[...]

        @pl.when(front == 0)
        def _():
            def one(index, carry):
                rows = chunk(index)
                modal_map[rows, :] = dot_last(inverse[rows, :], modes[...]).astype(BF16)
                return carry

            lax.fori_loop(0, CHUNKS, one, 0)

        @pl.when(front > 0)
        def _():
            def one(index, carry):
                rows = chunk(index)
                modal_map[rows, :] = modes[:, rows].T
                return carry

            lax.fori_loop(0, CHUNKS, one, 0)

    def build_picks():
        mode_rows[own_part(front), :] = dot_last(pick[...], modes[...]).astype(BF16)

        def send(step, carry):
            copy_mode(step, front).start()
            return carry

        lax.fori_loop(1, FRONTS, send, 0)

        place = lax.broadcasted_iota(jnp.int32, (COLS, COLS), 0)
        target = (
            lax.shift_right_logical(place, 4) * (FRONTS * SHARE)
            + jnp.bitwise_and(place, 15)
            + front * SHARE
        )
        route[...] = (target == ids_ref[pl.ds(sub, 1), :]).astype(F32).astype(BF16)
        lane_place = lax.broadcasted_iota(jnp.int32, (128, COLS), 0)

        def fill_low(index, carry):
            ids = jnp.bitwise_and(ids_ref[pl.ds(index, 1), :], 127)
            low_pick[:, tile(index, COLS)] = (lane_place == ids).astype(F32).astype(BF16)
            return carry

        lax.fori_loop(0, SUBS, fill_low, 0)

    def forward(group):
        rows = rows_of(group)

        @pl.when(front > 2 * group)
        def _():
            for index in range(CHUNKS):
                columns = chunk_lanes(index)
                copy_fwd(group, index).wait_recv()
                part = dot_wide(solved_in[rows, columns], coupling_turned[columns, :])
                if index == 0:
                    gathered[...] = part
                elif index < CHUNKS - 1:
                    gathered[...] = gathered[...] + part
                else:
                    reduced[...] = (gathered[...] + part).astype(BF16)

            first = tile(2 * group, OWN)
            second = tile(2 * group + 1, OWN)
            for index in range(CHUNKS):
                columns = chunk_lanes(index)
                result = 0.0 - dot_wide(reduced[...], turned[:, columns])
                solved[first, columns] = result[:OWN].astype(BF16)
                kept = solved[second, columns].astype(F32)
                solved[second, columns] = jnp.where(front == 2 * group + 1, kept, result[OWN:]).astype(BF16)

                @pl.when(front < last)
                def _():
                    copy_fwd(group, index).start()

        @pl.when(jnp.logical_and(front == 2 * group, front > 0))
        def _():
            for index in range(CHUNKS):
                copy_fwd(group, index).start()

    def send_entries(half):
        columns = pl.ds(half * HALF, HALF)
        entries[half, own_part(front)] = dot_last(own[...], back[columns, :])
        for step in (4, 5, 3, 2, 6, 7, 1):
            copy_entry(half, step, front).start()

    def displace_rows(group):
        rows = rows_of(group)

        def one(index, carry):
            columns = tile(index, 2 * CHUNK)
            displaced[rows, columns] = dot_wide(back[rows, :], inverse[:, columns])
            return carry

        lax.fori_loop(0, CHUNKS // 2, one, 0)

    def backward(group):
        rows = rows_of(group)
        for index in range(CHUNKS):
            columns = chunk_lanes(index)

            @pl.when(front < last)
            def _():
                copy_bwd(group, index).wait_recv()

            upper = solved[rows, columns].astype(F32)
            lower = handed_in[rows, columns].astype(F32)
            back[rows, columns] = jnp.where(front == last, upper, upper - lower).astype(BF16)

            @pl.when(front > 0)
            def _():
                total = dot_wide(back[rows, columns], inverse[columns, :])
                if index > 0:
                    total = displaced[rows, :] + total
                displaced[rows, :] = total
                if index == CHUNKS - 1:
                    reduced[...] = total.astype(BF16)

            @pl.when(front == 0)
            def _():
                part = dot_wide(back[rows, columns], modal_map[columns, :])
                modal_out[rows, :] = part if index == 0 else modal_out[rows, :] + part

        @pl.when(front > 0)
        def _():
            for index in range(CHUNKS):
                columns = chunk_lanes(index)
                handed[rows, columns] = dot_wide(reduced[...], coupling[:, columns]).astype(BF16)
                copy_bwd(group, index).start()

            modal_out[rows, :] = dot_wide(reduced[...], modal_map[...])

        @pl.when(front < last)
        def _():
            copy_sum(group).wait_recv()
            modal_out[rows, :] = modal_out[rows, :] + modal_in[rows, :].astype(F32)

        @pl.when(front > 0)
        def _():
            modal_part[rows, :] = modal_out[rows, :].astype(BF16)
            copy_sum(group).start()

        @pl.when(front == 0)
        def _():
            modal[rows, :] = modal_out[rows, :].astype(BF16)
            for step in (4, 5, 3, 2, 6, 7, 1):
                copy_modal(group, step).start()

        @pl.when(jnp.logical_and(front == 0, group > 0))
        def _():
            displace_rows(group)

        @pl.when(group == 2)
        def _():
            send_entries(1)

    build_modal_at = jnp.where(
        front < 5, jnp.maximum(2 * front + 1, 5), jnp.where(front < last, 1, 0)
    )
    build_picks_at = jnp.where(front < 4, 9, 99)
    shift = jnp.where(front == last, 1, -1)

    def slot(moment, carry):
        @pl.when(moment == build_modal_at)
        def _():
            build_modal_map()

        @pl.when(moment == build_picks_at)
        def _():
            build_picks()

        even = lax.rem(moment, 2) == 0
        ahead = front - moment // 2
        behind = 15 - front - (moment + shift) // 2

        @pl.when(jnp.logical_and(even, jnp.logical_and(ahead >= 0, lax.rem(ahead + 32, 2) == 0)))
        def _():
            forward(ahead // 2)

        @pl.when(
            jnp.logical_and(
                jnp.logical_not(even),
                jnp.logical_and(
                    jnp.logical_and(behind >= 0, behind < 2 * GROUPS), lax.rem(behind + 32, 2) == 0
                ),
            )
        )
        def _():
            backward(behind // 2)

        return carry

    lax.fori_loop(0, 32, slot, 0)
    send_entries(0)

    @pl.when(front == 0)
    def _():
        displace_rows(0)

    @pl.when(front >= 4)
    def _():
        build_picks()

    real = slice(0, COLS)

    @pl.when(front > 0)
    def _():
        for group in range(GROUPS):
            copy_modal(group, 1).wait_recv()

    def wait_rows(step, carry):
        copy_mode(step, peer_front(step)).wait_recv()
        copy_entry(0, step, peer_front(step)).wait_recv()
        copy_entry(1, step, peer_front(step)).wait_recv()
        return carry

    lax.fori_loop(1, FRONTS, wait_rows, 0)
    projected = dot_last(mode_rows[...], modal[real, :])
    for half in range(2):
        lanes = slice(half * HALF, (half + 1) * HALF)
        flexible = (entries[half] - projected[:, lanes]).astype(BF16)
        rows_out[:, :, lanes] = dot(route[...], flexible).astype(BF16).reshape(SUBS, SHARE, HALF)

    def send_row(step, carry):
        copy_row(step, sub).start()
        return carry

    lax.fori_loop(1, subs, send_row, 0)
    rows_in[sub] = rows_out[sub]

    def deflate(index, carry):
        columns = chunk(index)
        attachment[:, columns] = (
            displaced[real, columns] - dot(modal[real, :], modes[:, columns])
        ).astype(BF16)
        return carry

    lax.fori_loop(0, CHUNKS, deflate, 0)
    store = pltpu.make_async_copy(attachment, attachment_hbm.at[0], store_sem.at[0])
    store.start()

    def wait_row(step, carry):
        copy_row(step, peer_sub(step)).wait_recv()
        return carry

    lax.fori_loop(1, subs, wait_row, 0)
    high_place = lax.broadcasted_iota(jnp.int32, (SUBS, SHARE, COLS), 0)
    for index in range(SUBS):
        level = lax.shift_right_logical(ids_ref[index : index + 1, :], 7)
        chosen = jnp.where(
            high_place == level[:, None, :], rows_in[index].astype(F32)[None, :, :], 0.0
        ).astype(BF16)
        placed[:, index * COLS : (index + 1) * COLS] = chosen.reshape(SUBS * SHARE, COLS)
    total = dot_last(placed[...], low_pick[...])
    for index in range(SUBS):
        flexibility[:, index * 128 : (index + 1) * 128] = total[index * SHARE : (index + 1) * SHARE]
    store_flexibility = pltpu.make_async_copy(flexibility, flexibility_hbm, store_sem.at[1])
    store_flexibility.start()

    for group in range(GROUPS):

        @pl.when(jnp.logical_and(front < last, front >= 2 * group))
        def _():
            copy_fwd(group, 0, whole).wait_send()

        @pl.when(front > 0)
        def _():
            copy_bwd(group, 0, whole).wait_send()
            copy_sum(group).wait_send()

        @pl.when(front == 0)
        def _():
            for step in range(1, FRONTS):
                copy_modal(group, step).wait_send()

    def wait_sends(step, carry):
        copy_mode(step, front).wait_send()
        copy_entry(0, step, front).wait_send()
        copy_entry(1, step, front).wait_send()
        return carry

    lax.fori_loop(1, FRONTS, wait_sends, 0)

    def wait_row_sends(step, carry):
        copy_row(step, sub).wait_send()
        return carry

    lax.fori_loop(1, subs, wait_row_sends, 0)
    store.wait()
    store_flexibility.wait()


def on_device(front_inverse, coupling, free_modes, dof_offset, interface_id):
    dma = pltpu.SemaphoreType.DMA
    vmem = pltpu.VMEM
    anywhere = pl.BlockSpec(memory_space=pl.ANY)
    local = pl.BlockSpec(memory_space=pltpu.VMEM)
    return pl.pallas_call(
        kernel,
        out_shape=(
            jax.ShapeDtypeStruct((1, COLS, NF), BF16),
            jax.ShapeDtypeStruct((SHARE, NF), F32),
        ),
        in_specs=[anywhere, anywhere, anywhere, local, local],
        out_specs=(anywhere, anywhere),
        scratch_shapes=[
            vmem((NF, NF), BF16),
            vmem((NF, NF), BF16),
            vmem((MODES, NF), BF16),
            vmem((MPAD, NF), BF16),
            vmem((NF, NF), BF16),
            vmem((NF, NF), BF16),
            vmem((NF, MPAD), BF16),
            vmem((WIDTH, NF), F32),
            vmem((OWN, NF), BF16),
            vmem((OWN, NF), BF16),
            vmem((COLS, NF), BF16),
            vmem((COLS, NF), BF16),
            vmem((WIDTH, NF), BF16),
            vmem((COLS, NF), BF16),
            vmem((COLS, NF), BF16),
            vmem((COLS, NF), BF16),
            vmem((COLS, MPAD), F32),
            vmem((COLS, MPAD), BF16),
            vmem((COLS, MPAD), BF16),
            vmem((COLS, MPAD), BF16),
            vmem((COLS, MPAD), BF16),
            vmem((2, COLS, HALF), F32),
            vmem((COLS, COLS), BF16),
            vmem((SUBS, SHARE, COLS), BF16),
            vmem((SUBS, SHARE, COLS), BF16),
            vmem((128, SUBS * COLS), BF16),
            vmem((SUBS * SHARE, SUBS * COLS), BF16),
            vmem((COLS, NF), F32),
            vmem((COLS, NF), BF16),
            vmem((SHARE, NF), F32),
            dma((CHUNKS,)),
            dma((CHUNKS,)),
            dma,
            dma((GROUPS,)),
            dma((GROUPS, CHUNKS)),
            dma((GROUPS,)),
            dma((GROUPS, CHUNKS)),
            dma((GROUPS,)),
            dma((GROUPS,)),
            dma((GROUPS, FRONTS)),
            dma((GROUPS,)),
            dma((FRONTS,)),
            dma((FRONTS,)),
            dma((2, FRONTS)),
            dma((2, FRONTS)),
            dma((SUBS,)),
            dma((SUBS,)),
            dma((2,)),
        ],
        compiler_params=pltpu.CompilerParams(
            collective_id=0, has_side_effects=True, vmem_limit_bytes=60 << 20
        ),
        name="chain",
    )(front_inverse, coupling, free_modes, dof_offset, interface_id)


def solution(mesh):
    return jax.shard_map(
        on_device,
        mesh=mesh,
        in_specs=(
            P("sub", "front", None),
            P("sub", "front", None),
            P("sub", None, "front"),
            P("sub", "front"),
            P(),
        ),
        out_specs=(P("sub", None, "front"), P(("sub", "front"), None)),
        check_vma=False,
    )
```
